128 devices in a mesh: pair: 32 (over x, y, core), slab: 4 (over z).
Axes of the slice: x: 4, y: 4, z: 4, core: 2. Of those that a mesh axis runs over, the one named last changes fastest.
Arguments:
- amplitudes: bfloat16 [32, 32, 160000], P('pair'), may hold values from -6 to 6
- integrals: bfloat16 [160000, 1024], P('pair', 'slab'), may hold values from -0.0390625 to 0.0390625
- virt_irrep: int32 [400], replicated, may hold values from 0 to 7
- occ_energy: float32 [32], replicated, may hold values from -1.2 to -0.3
- slab_energy: float32 [32], replicated, may hold values from 0.1 to 1.5
Outputs:
- update: float32 [32, 32, 32, 32], P('pair', None, 'slab')
The draws below stay inside these ranges and needn't reach their ends.
All inputs are finite; a program needn't handle non-finite values.
Results may differ from the reference program's by a relative error of at most 0.0003.
Values may be sent and summed in bfloat16 or wider, within the bound.
A program may use at most 256 MiB of HBM per device.

```python
import jax
import jax.numpy as jnp
from jax import lax

V = 400
VS = 32
OCC = 32


def plant(values, key, least, high):
    dims = values.shape
    index_at = [jax.random.randint(jax.random.fold_in(key, axis), (), 0, dims[axis]) for axis in range(len(dims))]
    values = values.at[tuple(index_at)].set(least)
    longest = dims.index(max(dims))
    index_at[longest] = (index_at[longest] + 1) % dims[longest]
    return values.at[tuple(index_at)].set(high)


def level_of(key, dims, pieces, low, high):
    factor_of = 1.0
    for dim, parts in pieces:
        draws = jax.random.uniform(jax.random.fold_in(jax.random.fold_in(key, 6), dim), (parts,), jnp.float32, low / len(pieces), high / len(pieces))
        factor_of = factor_of * jnp.repeat(jnp.exp(draws), dims[dim] // parts).reshape((-1,) + (1,) * (len(dims) - 1 - dim))
    return factor_of


def centred(rng, shape, width, limit, pieces=(), kind=jnp.bfloat16):
    entries = width * jax.random.normal(rng, shape, jnp.float32)
    if pieces:
        entries = entries * level_of(rng, shape, pieces, -0.22, 0.18)
    return jnp.clip(entries, -limit, limit).astype(kind)


def setup_inputs(seed: int = 0) -> dict:
    seeds = jax.random.split(jax.random.key(seed), 6)
    amplitudes = centred(seeds[0], (OCC, OCC, V * V), 1.0, 6.0, ((0, 32),))
    integrals = centred(seeds[1], (V * V, VS * VS), (V * V // 8) ** -0.5, 0.0390625, ((0, 32), (1, 4)))
    virt_irrep = plant(jax.random.randint(seeds[2], (V,), 0, 8), jax.random.fold_in(seeds[2], 1), 0, 7).astype(jnp.int32)
    occ_energy = jnp.clip(jax.random.uniform(seeds[3], (OCC,), jnp.float32, -1.2, -0.3), -1.2, -0.3)
    slab_energy = jnp.clip(jax.random.uniform(seeds[4], (VS,), jnp.float32, 0.1, 1.5), 0.1, 1.5)
    return {"amplitudes": amplitudes, "integrals": integrals, "virt_irrep": virt_irrep, "occ_energy": occ_energy, "slab_energy": slab_energy}


def reference(amplitudes, integrals, virt_irrep, occ_energy, slab_energy):
    pair_total = OCC * OCC
    flat_amps = amplitudes.reshape(pair_total, V * V)
    irrep_cd = jnp.bitwise_xor(virt_irrep[:, None], virt_irrep[None, :]).reshape(V * V)
    slab_irrep = virt_irrep[:VS]
    irrep_ab = jnp.bitwise_xor(slab_irrep[:, None], slab_irrep[None, :]).reshape(VS * VS)
    block_rows = 16 * V

    def accumulate(carry, block_index):
        offset = (block_index * block_rows).astype(jnp.int32)
        amps_block = lax.dynamic_slice_in_dim(flat_amps, offset, block_rows, 1).astype(jnp.float32)
        ints_block = lax.dynamic_slice_in_dim(integrals, offset, block_rows, 0).astype(jnp.float32)
        rows_irrep = lax.dynamic_slice_in_dim(irrep_cd, offset, block_rows, 0)
        allowed = rows_irrep[:, None] == irrep_ab[None, :]
        ints_block = jnp.where(allowed, ints_block, jnp.zeros_like(ints_block))
        return carry + jnp.dot(amps_block, ints_block, preferred_element_type=jnp.float32), None

    ladder, _ = lax.scan(accumulate, jnp.zeros((pair_total, VS * VS), jnp.float32),
                         jnp.arange(V * V // block_rows, dtype=jnp.int32))
    residual = ladder.reshape(OCC, OCC, VS, VS)
    symmetric = residual + jnp.transpose(residual, (1, 0, 3, 2))
    denominator = (slab_energy[None, None, :, None] + slab_energy[None, None, None, :]
                   - occ_energy[:, None, None, None] - occ_energy[None, :, None, None])
    return symmetric / denominator
```

```python
import jax
import jax.numpy as jnp
from jax import lax
from jax.experimental import pallas as pl
from jax.experimental.pallas import tpu as pltpu
from jax.sharding import PartitionSpec as P

F32, BF16, I32 = jnp.float32, jnp.bfloat16, jnp.int32
V, VS, OCC = 400, 32, 32
NZ = 4
ROWS = 5000
GROUPS = ROWS // 8
LANES = 1280
CHUNKS = ((0, 512), (512, 512), (1024, 256))
MARGIN = 16
PARTS = (
    (0, 24, 0, 128, ("z", "x", "y")),
    (0, 24, 128, 128, ("x", "y", "z")),
    (24, 8, 0, 256, ("y", "z", "x")),
)
STEP_DIMS = ((4, 4), (4,), ())


def shift(i, d, n):
    return lax.rem(i + d, n)


def remote(src, dst, send, recv, pair, slab):
    return pltpu.make_async_remote_copy(
        src_ref=src, dst_ref=dst, send_sem=send, recv_sem=recv,
        device_id={"pair": pair, "slab": slab}, device_id_type=pl.DeviceIdType.MESH,
    )


def settle(ref, sem):
    pltpu.make_async_copy(ref, ref, sem).wait()


def kernel(amps, ints, irrep, out, *refs):
    nk = len(CHUNKS)
    abuf, bbuf = refs[:nk], refs[nk:2 * nk]
    bm, bp, perm, vrow, rowirr, colirr, c_ref, d_ref, r_ref = refs[2 * nk:2 * nk + 9]
    q = refs[2 * nk + 9:2 * nk + 18]
    a_send, b_send, a_recv, b_recv, own_sem, m_send, m_recv, q_send, q_recv = refs[2 * nk + 18:]

    p = lax.axis_index("pair")
    s = lax.axis_index("slab")
    x, y, c = p // 8, lax.rem(p // 2, 4), lax.rem(p, 2)

    def pair_at(dx, dy, dc):
        return shift(x, dx, 4) * 8 + shift(y, dy, 4) * 2 + shift(c, dc, 2)

    barrier = pltpu.get_barrier_semaphore()

    def greet(m, carry):
        pl.semaphore_signal(
            barrier, inc=1, device_id={"pair": shift(p, m, 32), "slab": s},
            device_id_type=pl.DeviceIdType.MESH,
        )
        return carry

    lax.fori_loop(1, 32, greet, 0)
    for dz in (1, 2, 3):
        pl.semaphore_signal(
            barrier, inc=1, device_id={"pair": p, "slab": shift(s, dz, NZ)},
            device_id_type=pl.DeviceIdType.MESH,
        )
    pl.semaphore_wait(barrier, 34)

    first_tile = ROWS * p // 128
    lead = lax.rem(p, 16)

    def columns(pair, k):
        tile = ROWS * pair // 128 + 10 * s
        return pl.ds(pl.multiple_of(tile * 128 + CHUNKS[k][0], 128), CHUNKS[k][1])

    def rows_for(slab, k):
        size = CHUNKS[k][1] // 8
        want = 160 * slab - lead + CHUNKS[k][0] // 8
        have = jnp.clip(want, 0, GROUPS - size)
        return pl.ds(have, size), pl.ds(MARGIN + have - want, size)

    def send_amps(k, dx, dy, dc):
        peer = pair_at(dx, dy, dc)
        remote(
            amps.at[:, columns(peer, k)], abuf[k].at[p], a_send, a_recv.at[k], peer, s
        ).start()

    own = []
    for k in range(nk):
        for dz in (1, 3, 2):
            slab = shift(s, dz, NZ)
            source, target = rows_for(slab, k)
            remote(
                ints.at[source], bbuf[k].at[s, target], b_send, b_recv.at[k], p, slab
            ).start()
        source, target = rows_for(s, k)
        own.append(pltpu.make_async_copy(ints.at[source], bbuf[k].at[s, target], own_sem.at[k, 0]))
        own.append(pltpu.make_async_copy(amps.at[:, columns(p, k)], abuf[k].at[p], own_sem.at[k, 1]))
        own[-2].start()
        own[-1].start()
        for dx in (1, 3, 2):
            send_amps(k, dx, dx, 0)

        def send_some(i, carry):
            for dx in (1, 3, 2, 0):
                send_amps(k, dx, i // 2 + dx, lax.rem(i, 2))
            return carry

        lax.fori_loop(1, 8, send_some, 0)

    def fill_perm(t, carry):
        row = lax.broadcasted_iota(I32, (128, 1024), 0) + t * 128
        col = lax.broadcasted_iota(I32, (128, 1024), 1)
        swapped = ((row & 31) << 5) | (row >> 5)
        perm[pl.ds(pl.multiple_of(t * 128, 128), 128), :] = jnp.where(
            swapped == col, F32(1), F32(0)
        ).astype(BF16)
        return carry

    lax.fori_loop(0, 8, fill_perm, 0)
    vrow[...] = jnp.zeros_like(vrow)
    vrow[0:1, 0:V] = irrep[...].astype(F32)
    table = jnp.broadcast_to(vrow[0:1, :], (128, 512)).astype(BF16)
    orb = lax.broadcasted_iota(I32, (128, 1024), 0)
    col = lax.broadcasted_iota(I32, (128, 1024), 1)

    def look_up(lhs, rhs, dims):
        return lax.dot_general(
            lhs, rhs, (dims, ((), ())), preferred_element_type=F32
        ).astype(I32)

    small = table[0:16, 0:128]
    of_a = look_up(small, jnp.where(orb == (col >> 5), F32(1), F32(0)).astype(BF16), ((1,), (0,)))
    of_b = look_up(small, jnp.where(orb == (col & 31), F32(1), F32(0)).astype(BF16), ((1,), (0,)))
    colirr[...] = (of_a ^ of_b)[0:8]

    start = (first_tile + 10 * s) * 128

    def fill_rows(t, carry):
        base = start + t * 256
        c0 = base // V
        row = lax.broadcasted_iota(I32, (256, 512), 0) + base
        orb = lax.broadcasted_iota(I32, (256, 512), 1)
        cc = jnp.where(row >= (c0 + 1) * V, c0 + 1, c0)
        dd = row - cc * V
        of_c = look_up(jnp.where(orb == cc, F32(1), F32(0)).astype(BF16), table, ((1,), (1,)))
        of_d = look_up(jnp.where(orb == dd, F32(1), F32(0)).astype(BF16), table, ((1,), (1,)))
        row = row[:, 0:128]
        inside = (row >= ROWS * p) & (row < ROWS * p + ROWS)
        rowirr[pl.ds(pl.multiple_of(t * 256, 256), 256), :] = jnp.where(inside, of_c ^ of_d, -1)
        return carry

    lax.fori_loop(0, LANES // 256, fill_rows, 0)

    for k, (offset, size) in enumerate(CHUNKS):
        settle(bbuf[k].at[pl.ds(0, 3), pl.ds(0, size // 8)], b_recv.at[k])
        own[2 * k].wait()

        def mask(t, carry):
            rows = pl.multiple_of(t * 128, 128)
            row_irrep = rowirr[pl.ds(offset + rows, 128), :]
            for block in range(8):
                slab, half = block // 2, block % 2
                part = bbuf[k][slab, pl.ds(MARGIN + t * 16, 16), :, pl.ds(half * 128, 128)]
                part = part.astype(F32).reshape(128, 128)
                keep = row_irrep == colirr[0:1, block * 128:block * 128 + 128]
                bm[pl.ds(rows, 128), block * 128:block * 128 + 128] = jnp.where(
                    keep, part, F32(0)
                ).astype(BF16)
            bp[pl.ds(rows, 128), :] = jnp.dot(
                bm[pl.ds(rows, 128), :], perm[...], preferred_element_type=F32
            ).astype(BF16)
            return carry

        lax.fori_loop(0, size // 128, mask, 0)
        settle(abuf[k].at[pl.ds(0, 31)], a_recv.at[k])
        own[2 * k + 1].wait()

        def multiply(t, carry):
            left = abuf[k][pl.ds(t * 8, 8)].reshape(256, size)
            for slab in range(NZ):
                cols = slice(slab * 256, slab * 256 + 256)
                direct = jnp.dot(left, bm[0:size, cols], preferred_element_type=F32)
                direct = direct.reshape(4, 2, 32, 256)
                mirror = jnp.dot(left, bp[0:size, cols], preferred_element_type=F32)
                rows = pl.ds(pl.multiple_of(t * 256, 256), 256)
                if k:
                    c_ref[slab, t] += direct
                    d_ref[2 * slab, rows] += mirror[:, 0:128]
                    d_ref[2 * slab + 1, rows] += mirror[:, 128:256]
                else:
                    c_ref[slab, t] = direct
                    d_ref[2 * slab, rows] = mirror[:, 0:128]
                    d_ref[2 * slab + 1, rows] = mirror[:, 128:256]
            return carry

        lax.fori_loop(0, 4, multiply, 0)

    merges = []
    sibling = pair_at(0, 0, 1)
    for slab in range(NZ):
        def join(m, carry):
            for core in range(2):
                for half in range(2):
                    mirrored = d_ref[2 * slab + half, pl.ds(2 * m + core, 32, stride=32), :]
                    c_ref[slab, m // 4, lax.rem(m, 4), core, :, half * 128:half * 128 + 128] += mirrored
            return carry

        lax.fori_loop(0, 16, join, 0)
        merges.append(
            remote(
                c_ref.at[slab, :, :, 1 - c], r_ref.at[slab], m_send.at[slab], m_recv.at[slab],
                sibling, s,
            )
        )
        merges[-1].start()
    for slab in range(NZ):
        merges[slab].wait_recv()

        def merge(m, carry):
            r_ref[slab, m // 4, lax.rem(m, 4)] += c_ref[slab, m // 4, lax.rem(m, 4), c]
            return carry

        lax.fori_loop(0, 16, merge, 0)

    place = {"z": s, "x": x, "y": y}

    for step in range(3):
        for part, (row, rows, lane, lanes, order) in enumerate(PARTS):
            axis = order[step]
            done = order[:step]
            for d in (1, 3, 2):
                target = shift(place[axis], d, 4)
                fixed = {a: place[a] for a in done}
                fixed[axis] = target
                index = tuple(
                    fixed[a] if a in fixed else slice(None) for a in ("z", "x", "y")
                )
                peer = p
                slab = s
                if axis == "x":
                    peer = target * 8 + y * 2 + c
                elif axis == "y":
                    peer = x * 8 + target * 2 + c
                else:
                    slab = target
                remote(
                    r5_at(r_ref, index, row, rows, lane, lanes),
                    q[3 * part + step].at[d - 1],
                    q_send.at[part, step], q_recv.at[part, step], peer, slab,
                ).start()
        for part, (row, rows, lane, lanes, order) in enumerate(PARTS):
            buffer = q[3 * part + step]
            settle(buffer, q_recv.at[part, step])
            fixed = {a: place[a] for a in order[:step + 1]}
            free = [a for a in ("z", "x", "y") if a not in fixed]

            def add(t, carry):
                spots = {}
                rest = t
                for a in reversed(free):
                    spots[a] = lax.rem(rest, 4)
                    rest = rest // 4
                where = tuple(fixed[a] if a in fixed else spots[a] for a in ("z", "x", "y"))
                spot = tuple(spots[a] for a in free)
                mine = r5_at(r_ref, where, row, rows, lane, lanes)
                total = mine[...]
                for d in range(3):
                    total = total + buffer[(d, *spot)]
                if step == 2:
                    out[pl.ds(row, rows), pl.ds(lane, lanes)] = total
                else:
                    mine[...] = total
                return carry

            if free:
                lax.fori_loop(0, 4 ** len(free), add, 0)
            else:
                add(0, 0)

    for k in range(nk):
        settle(abuf[k].at[pl.ds(0, 31)], a_send)
        settle(bbuf[k].at[pl.ds(0, 3), pl.ds(0, CHUNKS[k][1] // 8)], b_send)
    for slab in range(NZ):
        merges[slab].wait_send()
    for part in range(3):
        for step in range(3):
            settle(q[3 * part + step], q_send.at[part, step])


def r5_at(ref, index, row, rows, lane, lanes):
    z, x, y = index
    return ref.at[z, x, y, pl.ds(row, rows), pl.ds(lane, lanes)]


def contract(amps, ints, irrep):
    nk = len(CHUNKS)
    dma = pltpu.SemaphoreType.DMA
    scratch = [pltpu.VMEM((OCC, 32, size), BF16) for _, size in CHUNKS]
    scratch += [pltpu.VMEM((NZ, size // 8 + 2 * MARGIN, 8, 256), BF16) for _, size in CHUNKS]
    widest = max(size for _, size in CHUNKS)
    scratch += [
        pltpu.VMEM((widest, 1024), BF16),
        pltpu.VMEM((widest, 1024), BF16),
        pltpu.VMEM((1024, 1024), BF16),
        pltpu.VMEM((8, 512), F32),
        pltpu.VMEM((LANES, 128), I32),
        pltpu.VMEM((8, 1024), I32),
        pltpu.VMEM((NZ, 4, 4, 2, 32, 256), F32),
        pltpu.VMEM((2 * NZ, 1024, 128), F32),
        pltpu.VMEM((NZ, 4, 4, 32, 256), F32),
    ]
    for row, rows, lane, lanes, _ in PARTS:
        for dims in STEP_DIMS:
            scratch.append(pltpu.VMEM((3, *dims, rows, lanes), F32))
    scratch += [
        dma, dma, dma((nk,)), dma((nk,)), dma((nk, 2)), dma((NZ,)), dma((NZ,)), dma((3, 3)), dma((3, 3)),
    ]
    return pl.pallas_call(
        kernel,
        out_shape=jax.ShapeDtypeStruct((32, 256), F32),
        in_specs=[
            pl.BlockSpec(memory_space=pltpu.HBM),
            pl.BlockSpec(memory_space=pltpu.HBM),
            pl.BlockSpec(memory_space=pltpu.VMEM),
        ],
        out_specs=pl.BlockSpec(memory_space=pltpu.VMEM),
        scratch_shapes=scratch,
        compiler_params=pltpu.CompilerParams(
            collective_id=0, has_side_effects=True, vmem_limit_bytes=52 << 20
        ),
    )(amps, ints, irrep)


def local(amplitudes, integrals, virt_irrep, occ_energy, slab_energy):
    pair_index = lax.axis_index("pair")
    slab_index = lax.axis_index("slab")
    summed = contract(
        amplitudes.reshape(OCC, V * V), integrals.reshape(GROUPS, 8, 256), virt_irrep.reshape(1, V)
    )
    symmetric = summed.reshape(1, OCC, VS // NZ, VS)
    energy_i = lax.dynamic_slice_in_dim(occ_energy, pair_index, 1, 0)
    energy_a = lax.dynamic_slice_in_dim(slab_energy, slab_index * (VS // NZ), VS // NZ, 0)
    denominator = (
        energy_a[None, None, :, None]
        + slab_energy[None, None, None, :]
        - energy_i[:, None, None, None]
        - occ_energy[None, :, None, None]
    )
    return symmetric / denominator


def solution(mesh):
    placed = (P("pair", None, None), P("pair", "slab"), P(), P(), P())
    return jax.shard_map(
        local, mesh=mesh, in_specs=placed, out_specs=P("pair", None, "slab", None), check_vma=False
    )
```

```python
import jax
import jax.numpy as jnp
from jax import lax
from jax.experimental import pallas as pl
from jax.experimental.pallas import tpu as pltpu
from jax.sharding import PartitionSpec as P

F32, BF16, I32 = jnp.float32, jnp.bfloat16, jnp.int32
V, VS, OCC = 400, 32, 32
NZ = 4
ROWS = 5000
GROUPS = ROWS // 8
LANES = 1280
CHUNKS = ((0, 512), (512, 512), (1024, 256))
MARGIN = 16
PARTS = (
    (0, 24, 0, 128, ("z", "x", "y")),
    (0, 24, 128, 128, ("x", "y", "z")),
    (24, 8, 0, 256, ("y", "z", "x")),
)
STEP_DIMS = ((4, 4), (4,), ())
AXES = ("z", "x", "y")


def shift(i, d, n):
    return lax.rem(i + d, n)


def remote(src, dst, send, recv, pair, slab):
    return pltpu.make_async_remote_copy(
        src_ref=src, dst_ref=dst, send_sem=send, recv_sem=recv,
        device_id={"pair": pair, "slab": slab}, device_id_type=pl.DeviceIdType.MESH,
    )


def settle(ref, sem):
    pltpu.make_async_copy(ref, ref, sem).wait()


def one_hot(test):
    return jnp.where(test, F32(1), F32(0)).astype(BF16)


def kernel(amps, ints, irrep, occ, virt, out, *refs):
    nk = len(CHUNKS)
    abuf, bbuf = refs[:nk], refs[nk:2 * nk]
    refs = refs[2 * nk:]
    ap, bm, bp, perm, vrow, rowirr, colirr, den, fin, c_ref, r_ref = refs[:11]
    irrep_v, occ_s, virt_s = refs[11:14]
    q = refs[14:23]
    a_send, b_send, a_recv, b_recv, own_sem, arg_sem, m_send, m_recv, q_send, q_recv = refs[23:]

    p = lax.axis_index("pair")
    s = lax.axis_index("slab")
    x, y, c = p // 8, lax.rem(p // 2, 4), lax.rem(p, 2)
    place = {"z": s, "x": x, "y": y}

    def pair_at(dx, dy, dc):
        return shift(x, dx, 4) * 8 + shift(y, dy, 4) * 2 + shift(c, dc, 2)

    barrier = pltpu.get_barrier_semaphore()

    def greet(pair, slab):
        pl.semaphore_signal(
            barrier, inc=1, device_id={"pair": pair, "slab": slab},
            device_id_type=pl.DeviceIdType.MESH,
        )

    def greet_some(i, carry):
        for dx in (2, 1, 3, 0):
            greet(pair_at(dx, i // 2 + dx, lax.rem(i, 2)), s)
        return carry

    for dx in (2, 1, 3):
        greet(pair_at(dx, dx, 0), s)
    lax.fori_loop(1, 8, greet_some, 0)
    for dz in (2, 1, 3):
        greet(p, shift(s, dz, NZ))
    small = [
        pltpu.make_async_copy(src, dst, arg_sem.at[i])
        for i, (src, dst) in enumerate(((irrep, irrep_v), (occ, occ_s), (virt, virt_s)))
    ]
    for copy in small:
        copy.start()
    pl.semaphore_wait(barrier, 34)

    first_tile = ROWS * p // 128
    lead = lax.rem(p, 16)

    def columns(pair, k):
        tile = ROWS * pair // 128 + 10 * s
        return pl.ds(pl.multiple_of(tile * 128 + CHUNKS[k][0], 128), CHUNKS[k][1])

    def rows_for(slab, k):
        size = CHUNKS[k][1] // 8
        want = 160 * slab - lead + CHUNKS[k][0] // 8
        have = jnp.clip(want, 0, GROUPS - size)
        return pl.ds(have, size), pl.ds(MARGIN + have - want, size)

    def send_amps(k, dx, dy, dc):
        peer = pair_at(dx, dy, dc)
        remote(
            amps.at[:, columns(peer, k)], abuf[k].at[p], a_send, a_recv.at[k], peer, s
        ).start()

    own = []
    for k in range(nk):
        for dz in (1, 3, 2):
            slab = shift(s, dz, NZ)
            source, target = rows_for(slab, k)
            remote(
                ints.at[source], bbuf[k].at[s, target], b_send, b_recv.at[k], p, slab
            ).start()
        source, target = rows_for(s, k)
        own.append(pltpu.make_async_copy(ints.at[source], bbuf[k].at[s, target], own_sem.at[k, 0]))
        own.append(pltpu.make_async_copy(amps.at[:, columns(p, k)], abuf[k].at[p], own_sem.at[k, 1]))
        for dx in (1, 3, 2):
            send_amps(k, dx, dx, 0)

        def send_some(i, carry):
            for dx in (1, 3, 2, 0):
                send_amps(k, dx, i // 2 + dx, lax.rem(i, 2))
            return carry

        lax.fori_loop(1, 8, send_some, 0)
    for copy in own:
        copy.start()

    def fill_perm(t, carry):
        row = lax.broadcasted_iota(I32, (128, 1024), 0) + t * 128
        col = lax.broadcasted_iota(I32, (128, 1024), 1)
        swapped = ((row & 31) << 5) | (row >> 5)
        perm[pl.ds(pl.multiple_of(t * 128, 128), 128), :] = one_hot(swapped == col)
        return carry

    lax.fori_loop(0, 8, fill_perm, 0)
    for copy in small:
        copy.wait()

    vrow[...] = jnp.zeros_like(vrow)
    vrow[0:1, 0:V] = irrep_v[...].astype(F32)
    table = jnp.broadcast_to(vrow[0:1, :], (128, 512)).astype(BF16)

    def look_up(lhs, rhs, dims):
        return lax.dot_general(
            lhs, rhs, (dims, ((), ())), preferred_element_type=F32
        ).astype(I32)

    orb = lax.broadcasted_iota(I32, (128, 1024), 0)
    col = lax.broadcasted_iota(I32, (128, 1024), 1)
    first = table[0:16, 0:128]
    of_a = look_up(first, one_hot(orb == (col >> 5)), ((1,), (0,)))
    of_b = look_up(first, one_hot(orb == (col & 31)), ((1,), (0,)))
    colirr[...] = (of_a ^ of_b)[0:8]

    start = (first_tile + 10 * s) * 128

    def fill_rows(t, carry):
        base = start + t * 256
        c0 = base // V
        row = lax.broadcasted_iota(I32, (256, 512), 0) + base
        orb = lax.broadcasted_iota(I32, (256, 512), 1)
        cc = jnp.where(row >= (c0 + 1) * V, c0 + 1, c0)
        of_c = look_up(one_hot(orb == cc), table, ((1,), (1,)))
        of_d = look_up(one_hot(orb == row - cc * V), table, ((1,), (1,)))
        row = row[:, 0:128]
        inside = (row >= ROWS * p) & (row < ROWS * p + ROWS)
        rowirr[pl.ds(pl.multiple_of(t * 256, 256), 256), :] = jnp.where(inside, of_c ^ of_d, -1)
        return carry

    lax.fori_loop(0, LANES // 256, fill_rows, 0)

    lane = lax.broadcasted_iota(I32, (8, 256), 1)
    row = lax.broadcasted_iota(I32, (32, 256), 0)
    of_a = jnp.zeros((8, 256), F32)
    of_b = jnp.zeros((8, 256), F32)
    of_j = jnp.zeros((32, 256), F32)
    for i in range(VS // NZ):
        of_a = jnp.where((lane >> 5) == i, virt_s[0, s * (VS // NZ) + i], of_a)
    for i in range(VS):
        of_b = jnp.where((lane & 31) == i, virt_s[0, i], of_b)
    for i in range(OCC):
        of_j = jnp.where(row == i, occ_s[0, i], of_j)
    den[...] = ((of_a + of_b) - occ_s[0, p])[0:1] - of_j

    merges = []
    sibling = pair_at(0, 0, 1)
    for k, (offset, size) in enumerate(CHUNKS):
        settle(bbuf[k].at[pl.ds(0, 3), pl.ds(0, size // 8)], b_recv.at[k])
        own[2 * k].wait()

        def mask(t, carry):
            rows = pl.multiple_of(t * 128, 128)
            row_irrep = rowirr[pl.ds(offset + rows, 128), :]
            for block in range(8):
                slab, half = block // 2, block % 2
                part = bbuf[k][slab, pl.ds(MARGIN + t * 16, 16), :, pl.ds(half * 128, 128)]
                part = part.astype(F32).reshape(128, 128)
                keep = row_irrep == colirr[0:1, block * 128:block * 128 + 128]
                bm[pl.ds(rows, 128), block * 128:block * 128 + 128] = jnp.where(
                    keep, part, F32(0)
                ).astype(BF16)
            bp[pl.ds(rows, 128), :] = jnp.dot(
                bm[pl.ds(rows, 128), :], perm[...], preferred_element_type=F32
            ).astype(BF16)
            return carry

        lax.fori_loop(0, size // 128, mask, 0)
        settle(abuf[k].at[pl.ds(0, 31)], a_recv.at[k])
        own[2 * k + 1].wait()

        def mirror(t, carry):
            rows = pl.ds(pl.multiple_of(t * 256, 256), 256)
            ap[rows, 0:size] = jnp.dot(
                perm[rows, :], abuf[k][...].reshape(1024, size), preferred_element_type=F32
            ).astype(BF16)
            return carry

        lax.fori_loop(0, 4, mirror, 0)

        def multiply(t, slab):
            cols = pl.ds(pl.multiple_of(slab * 256, 256), 256)
            direct = jnp.dot(
                abuf[k][pl.ds(t * 8, 8)].reshape(256, size), bm[0:size, cols],
                preferred_element_type=F32,
            )
            swapped = jnp.dot(
                ap[pl.ds(pl.multiple_of(t * 256, 256), 256), 0:size], bp[0:size, cols],
                preferred_element_type=F32,
            )
            total = (direct + swapped).reshape(4, 2, 32, 256)
            if k:
                total = total + c_ref[slab, t]
            c_ref[slab, t] = total
            return slab

        if k < nk - 1:
            def multiply_all(i, carry):
                multiply(i // 4, lax.rem(i, 4))
                return carry

            lax.fori_loop(0, 16, multiply_all, 0)
        else:
            for n, dz in enumerate((2, 1, 3, 0)):
                slab = shift(s, dz, NZ)
                lax.fori_loop(0, 4, multiply, slab)
                merges.append(
                    remote(
                        c_ref.at[slab, :, :, 1 - c], r_ref.at[slab], m_send.at[n], m_recv.at[n],
                        sibling, s,
                    )
                )
                merges[-1].start()

    def block(index, part):
        row, rows, lane, lanes, _ = PARTS[part]
        return r_ref.at[(*index, pl.ds(row, rows), pl.ds(lane, lanes))]

    def hand_on(part, step, d, index, target, extra=()):
        axis = PARTS[part][4][step]
        at = {**place, axis: target}
        remote(
            block(index, part), q[3 * part + step].at[(d - 1, *extra)],
            q_send.at[part, step], q_recv.at[part, step],
            at["x"] * 8 + at["y"] * 2 + c, at["z"],
        ).start()

    every = slice(None)
    for n, dz in enumerate((2, 1, 3, 0)):
        slab = shift(s, dz, NZ)
        merges[n].wait_recv()

        def merge(m, carry):
            r_ref[slab, m // 4, lax.rem(m, 4)] += c_ref[slab, m // 4, lax.rem(m, 4), c]
            return carry

        lax.fori_loop(0, 16, merge, 0)
        if dz:
            hand_on(0, 0, dz, (slab, every, every), slab)
        for d in (1, 3, 2):
            target = shift(x, d, 4)
            hand_on(1, 0, d, (slab, target, every), target, (slab,))
            target = shift(y, d, 4)
            hand_on(2, 0, d, (slab, every, target), target, (slab,))

    for step in range(3):
        for part, (row, rows, lane, lanes, order) in enumerate(PARTS):
            buffer = q[3 * part + step]
            settle(buffer, q_recv.at[part, step])
            fixed = {a: place[a] for a in order[:step + 1]}
            free = [a for a in AXES if a not in fixed]

            def add(t, carry):
                spots = {}
                rest = t
                for a in reversed(free):
                    spots[a] = lax.rem(rest, 4)
                    rest = rest // 4
                mine = block([fixed[a] if a in fixed else spots[a] for a in AXES], part)
                total = mine[...]
                for d in range(3):
                    total = total + buffer[(d, *[spots[a] for a in free])]
                if step == 2:
                    fin[pl.ds(row, rows), pl.ds(lane, lanes)] = total
                else:
                    mine[...] = total
                return carry

            if free:
                lax.fori_loop(0, 4 ** len(free), add, 0)
            else:
                add(0, 0)
            if step < 2:
                axis = order[step + 1]
                for d in (1, 3, 2):
                    target = shift(place[axis], d, 4)
                    at = {**fixed, axis: target}
                    hand_on(part, step + 1, d, tuple(at.get(a, every) for a in AXES), target)

    fin[...] = fin[...] / den[...]
    for i in range(VS // NZ):
        out[pl.ds(i, 32, stride=VS // NZ), :] = fin[:, i * VS:i * VS + VS]

    for k in range(nk):
        settle(abuf[k].at[pl.ds(0, 31)], a_send)
        settle(bbuf[k].at[pl.ds(0, 3), pl.ds(0, CHUNKS[k][1] // 8)], b_send)
    for n in range(NZ):
        merges[n].wait_send()
    for part in range(3):
        for step in range(3):
            settle(q[3 * part + step], q_send.at[part, step])


def contract(amps, ints, irrep, occ, virt):
    nk = len(CHUNKS)
    dma = pltpu.SemaphoreType.DMA
    widest = max(size for _, size in CHUNKS)
    scratch = [pltpu.VMEM((OCC, 32, size), BF16) for _, size in CHUNKS]
    scratch += [pltpu.VMEM((NZ, size // 8 + 2 * MARGIN, 8, 256), BF16) for _, size in CHUNKS]
    scratch += [
        pltpu.VMEM((1024, widest), BF16),
        pltpu.VMEM((widest, 1024), BF16),
        pltpu.VMEM((widest, 1024), BF16),
        pltpu.VMEM((1024, 1024), BF16),
        pltpu.VMEM((8, 512), F32),
        pltpu.VMEM((LANES, 128), I32),
        pltpu.VMEM((8, 1024), I32),
        pltpu.VMEM((32, 256), F32),
        pltpu.VMEM((32, 256), F32),
        pltpu.VMEM((NZ, 4, 4, 2, 32, 256), F32),
        pltpu.VMEM((NZ, 4, 4, 32, 256), F32),
        pltpu.VMEM((1, V), I32),
        pltpu.SMEM((1, OCC), F32),
        pltpu.SMEM((1, VS), F32),
    ]
    for _, rows, _, lanes, _ in PARTS:
        for dims in STEP_DIMS:
            scratch.append(pltpu.VMEM((3, *dims, rows, lanes), F32))
    scratch += [
        dma, dma, dma((nk,)), dma((nk,)), dma((nk, 2)), dma((3,)), dma((NZ,)), dma((NZ,)),
        dma((3, 3)), dma((3, 3)),
    ]
    return pl.pallas_call(
        kernel,
        out_shape=jax.ShapeDtypeStruct((OCC * VS // NZ, VS), F32),
        in_specs=[pl.BlockSpec(memory_space=pltpu.HBM)] * 5,
        out_specs=pl.BlockSpec(memory_space=pltpu.VMEM),
        scratch_shapes=scratch,
        compiler_params=pltpu.CompilerParams(
            collective_id=0, has_side_effects=True, vmem_limit_bytes=52 << 20
        ),
    )(amps, ints, irrep, occ, virt)


def local(amplitudes, integrals, virt_irrep, occ_energy, slab_energy):
    update = contract(
        amplitudes.reshape(OCC, V * V), integrals.reshape(GROUPS, 8, 256),
        virt_irrep.reshape(1, V), occ_energy.reshape(1, OCC), slab_energy.reshape(1, VS),
    )
    return update.reshape(1, OCC, VS // NZ, VS)


def solution(mesh):
    placed = (P("pair", None, None), P("pair", "slab"), P(), P(), P())
    return jax.shard_map(
        local, mesh=mesh, in_specs=placed, out_specs=P("pair", None, "slab", None), check_vma=False
    )
```

```python
import jax
import jax.numpy as jnp
from jax import lax
from jax.experimental import pallas as pl
from jax.experimental.pallas import tpu as pltpu
from jax.sharding import PartitionSpec as P

F32, BF16, I32 = jnp.float32, jnp.bfloat16, jnp.int32
V, VS, OCC = 400, 32, 32
NZ = 4
ROWS = 5000
GROUPS = ROWS // 8
LANES = 1280
CHUNKS = ((0, 512), (512, 512), (1024, 256))
MARGIN = 16
PARTS = (
    (0, 24, 0, 128, ("z", "x", "y")),
    (0, 24, 128, 128, ("x", "y", "z")),
    (24, 8, 0, 256, ("y", "z", "x")),
)
STEP_DIMS = ((4, 4), (4,), ())
AXES = ("z", "x", "y")


def shift(i, d, n):
    return lax.rem(i + d, n)


def remote(src, dst, send, recv, pair, slab):
    return pltpu.make_async_remote_copy(
        src_ref=src, dst_ref=dst, send_sem=send, recv_sem=recv,
        device_id={"pair": pair, "slab": slab}, device_id_type=pl.DeviceIdType.MESH,
    )


def settle(ref, sem):
    pltpu.make_async_copy(ref, ref, sem).wait()


def one_hot(test):
    return jnp.where(test, F32(1), F32(0)).astype(BF16)


def kernel(amps, ints, irrep, occ, virt, out, *refs):
    nk = len(CHUNKS)
    abuf, bbuf = refs[:nk], refs[nk:2 * nk]
    refs = refs[2 * nk:]
    ap, bm, bp, perm_ij, perm_ab, vrow, rowirr, colirr, den, fin, c_ref, r_ref = refs[:12]
    irrep_v, occ_s, virt_s = refs[12:15]
    q = refs[15:24]
    a_send, b_send, a_recv, b_recv, own_sem, arg_sem, m_send, m_recv, q_send, q_recv = refs[24:]

    p = lax.axis_index("pair")
    s = lax.axis_index("slab")
    x, y, c = p // 8, lax.rem(p // 2, 4), lax.rem(p, 2)
    place = {"z": s, "x": x, "y": y}

    def pair_at(dx, dy, dc):
        return shift(x, dx, 4) * 8 + shift(y, dy, 4) * 2 + shift(c, dc, 2)

    barrier = pltpu.get_barrier_semaphore()

    def greet(pair, slab):
        pl.semaphore_signal(
            barrier, inc=1, device_id={"pair": pair, "slab": slab},
            device_id_type=pl.DeviceIdType.MESH,
        )

    def greet_some(i, carry):
        for dx in (2, 1, 3, 0):
            greet(pair_at(dx, i // 2 + dx, lax.rem(i, 2)), s)
        return carry

    for dx in (2, 1, 3):
        greet(pair_at(dx, dx, 0), s)
    lax.fori_loop(1, 8, greet_some, 0)
    for dz in (2, 1, 3):
        greet(p, shift(s, dz, NZ))
    small = [
        pltpu.make_async_copy(src, dst, arg_sem.at[i])
        for i, (src, dst) in enumerate(((irrep, irrep_v), (occ, occ_s), (virt, virt_s)))
    ]
    for copy in small:
        copy.start()
    pl.semaphore_wait(barrier, 34)

    first_tile = ROWS * p // 128
    lead = lax.rem(p, 16)

    def columns(pair, k):
        tile = ROWS * pair // 128 + 10 * s
        return pl.ds(pl.multiple_of(tile * 128 + CHUNKS[k][0], 128), CHUNKS[k][1])

    def rows_for(slab, k):
        size = CHUNKS[k][1] // 8
        want = 160 * slab - lead + CHUNKS[k][0] // 8
        have = jnp.clip(want, 0, GROUPS - size)
        return pl.ds(have, size), pl.ds(MARGIN + have - want, size)

    def send_amps(k, dx, dy, dc):
        peer = pair_at(dx, dy, dc)
        remote(
            amps.at[:, columns(peer, k)], abuf[k].at[p], a_send, a_recv.at[k], peer, s
        ).start()

    own = []
    for k in range(nk):
        for dz in (1, 3, 2):
            slab = shift(s, dz, NZ)
            source, target = rows_for(slab, k)
            remote(
                ints.at[source], bbuf[k].at[3 - dz, target], b_send, b_recv.at[k], p, slab
            ).start()
        source, target = rows_for(s, k)
        own.append(pltpu.make_async_copy(ints.at[source], bbuf[k].at[3, target], own_sem.at[k, 0]))
        own.append(pltpu.make_async_copy(amps.at[:, columns(p, k)], abuf[k].at[p], own_sem.at[k, 1]))
        for dx in (1, 3, 2):
            send_amps(k, dx, dx, 0)

        def send_some(i, carry):
            for dx in (1, 3, 2, 0):
                send_amps(k, dx, i // 2 + dx, lax.rem(i, 2))
            return carry

        lax.fori_loop(1, 8, send_some, 0)
    for copy in own:
        copy.start()

    def orbitals(col):
        return ((((col >> 8) + s + 1) & 3) << 3) | ((col >> 5) & 7), col & 31

    def fill_perm(t, carry):
        row = lax.broadcasted_iota(I32, (128, 1024), 0) + t * 128
        col = lax.broadcasted_iota(I32, (128, 1024), 1)
        rows = pl.ds(pl.multiple_of(t * 128, 128), 128)
        perm_ij[rows, :] = one_hot((((row & 31) << 5) | (row >> 5)) == col)
        a, b = orbitals(col)
        perm_ab[rows, :] = one_hot(
            row == (((((b >> 3) + 3 - s) & 3) << 8) | ((b & 7) << 5) | a)
        )
        return carry

    lax.fori_loop(0, 8, fill_perm, 0)
    for copy in small:
        copy.wait()

    vrow[...] = jnp.zeros_like(vrow)
    vrow[0:1, 0:V] = irrep_v[...].astype(F32)
    table = jnp.broadcast_to(vrow[0:1, :], (128, 512)).astype(BF16)

    def look_up(lhs, rhs, dims):
        return lax.dot_general(
            lhs, rhs, (dims, ((), ())), preferred_element_type=F32
        ).astype(I32)

    orb = lax.broadcasted_iota(I32, (128, 1024), 0)
    col = lax.broadcasted_iota(I32, (128, 1024), 1)
    first = table[0:16, 0:128]
    of_a, of_b = (look_up(first, one_hot(orb == v), ((1,), (0,))) for v in orbitals(col))
    colirr[...] = (of_a ^ of_b)[0:8]

    start = (first_tile + 10 * s) * 128

    def fill_rows(t, carry):
        base = start + t * 256
        c0 = base // V
        row = lax.broadcasted_iota(I32, (256, 512), 0) + base
        orb = lax.broadcasted_iota(I32, (256, 512), 1)
        cc = jnp.where(row >= (c0 + 1) * V, c0 + 1, c0)
        of_c = look_up(one_hot(orb == cc), table, ((1,), (1,)))
        of_d = look_up(one_hot(orb == row - cc * V), table, ((1,), (1,)))
        row = row[:, 0:128]
        inside = (row >= ROWS * p) & (row < ROWS * p + ROWS)
        rowirr[pl.ds(pl.multiple_of(t * 256, 256), 256), :] = jnp.where(inside, of_c ^ of_d, -1)
        return carry

    lax.fori_loop(0, LANES // 256, fill_rows, 0)

    lane = lax.broadcasted_iota(I32, (8, 256), 1)
    row = lax.broadcasted_iota(I32, (32, 256), 0)
    of_a = jnp.zeros((8, 256), F32)
    of_b = jnp.zeros((8, 256), F32)
    of_j = jnp.zeros((32, 256), F32)
    for i in range(VS // NZ):
        of_a = jnp.where((lane >> 5) == i, virt_s[0, s * (VS // NZ) + i], of_a)
    for i in range(VS):
        of_b = jnp.where((lane & 31) == i, virt_s[0, i], of_b)
    for i in range(OCC):
        of_j = jnp.where(row == i, occ_s[0, i], of_j)
    den[...] = ((of_a + of_b) - occ_s[0, p])[0:1] - of_j

    merges = []
    sibling = pair_at(0, 0, 1)
    for k, (offset, size) in enumerate(CHUNKS):
        settle(bbuf[k].at[pl.ds(0, 3), pl.ds(0, size // 8)], b_recv.at[k])
        own[2 * k].wait()

        def mask(t, carry):
            rows = pl.multiple_of(t * 128, 128)
            row_irrep = rowirr[pl.ds(offset + rows, 128), :]
            for block in range(8):
                slab, half = block // 2, block % 2
                part = bbuf[k][slab, pl.ds(MARGIN + t * 16, 16), :, pl.ds(half * 128, 128)]
                part = part.astype(F32).reshape(128, 128)
                keep = row_irrep == colirr[0:1, block * 128:block * 128 + 128]
                bm[pl.ds(rows, 128), block * 128:block * 128 + 128] = jnp.where(
                    keep, part, F32(0)
                ).astype(BF16)
            bp[pl.ds(rows, 128), :] = jnp.dot(
                bm[pl.ds(rows, 128), :], perm_ab[...], preferred_element_type=F32
            ).astype(BF16)
            return carry

        lax.fori_loop(0, size // 128, mask, 0)
        settle(abuf[k].at[pl.ds(0, 31)], a_recv.at[k])
        own[2 * k + 1].wait()

        def mirror(t, carry):
            rows = pl.ds(pl.multiple_of(t * 256, 256), 256)
            ap[rows, 0:size] = jnp.dot(
                perm_ij[rows, :], abuf[k][...].reshape(1024, size), preferred_element_type=F32
            ).astype(BF16)
            return carry

        lax.fori_loop(0, 4, mirror, 0)

        def multiply(t, n):
            cols = slice(n * 256, n * 256 + 256)
            direct = jnp.dot(
                abuf[k][pl.ds(t * 8, 8)].reshape(256, size), bm[0:size, cols],
                preferred_element_type=F32,
            )
            rows = t * 256 if isinstance(t, int) else pl.multiple_of(t * 256, 256)
            swapped = jnp.dot(
                ap[pl.ds(rows, 256), 0:size], bp[0:size, cols], preferred_element_type=F32
            )
            total = (direct + swapped).reshape(4, 2, 32, 256)
            if k:
                total = total + c_ref[n, t]
            c_ref[n, t] = total

        if k < nk - 1:
            def multiply_all(t, carry):
                for n in range(NZ):
                    multiply(t, n)
                return carry

            lax.fori_loop(0, 4, multiply_all, 0)
        else:
            for n in range(NZ):
                for t in range(4):
                    multiply(t, n)
                merges.append(
                    remote(
                        c_ref.at[n, :, :, 1 - c], r_ref.at[n], m_send.at[n], m_recv.at[n],
                        sibling, s,
                    )
                )
                merges[-1].start()

    own_at = {"z": 3, "x": x, "y": y}

    def block(index, part):
        row, rows, lane, lanes, _ = PARTS[part]
        return r_ref.at[(*index, pl.ds(row, rows), pl.ds(lane, lanes))]

    def hand_on(part, step, d, fixed, extra=()):
        axis = PARTS[part][4][step]
        target = shift(place[axis], d, 4)
        fixed = {**fixed, axis: d - 1 if axis == "z" else target}
        at = {**place, axis: target}
        remote(
            block([fixed.get(a, slice(None)) for a in AXES], part),
            q[3 * part + step].at[(d - 1, *extra)],
            q_send.at[part, step], q_recv.at[part, step],
            at["x"] * 8 + at["y"] * 2 + c, at["z"],
        ).start()

    for n in range(NZ):
        merges[n].wait_recv()

        def merge(m, carry):
            r_ref[n, m // 4, lax.rem(m, 4)] += c_ref[n, m // 4, lax.rem(m, 4), c]
            return carry

        lax.fori_loop(0, 16, merge, 0, unroll=4)
        for d in (2, 1, 3):
            if d == n + 1:
                hand_on(0, 0, d, {})
            hand_on(1, 0, d, {"z": n}, (n,))
            hand_on(2, 0, d, {"z": n}, (n,))

    for step in range(3):
        for part, (row, rows, lane, lanes, order) in enumerate(PARTS):
            buffer = q[3 * part + step]
            settle(buffer, q_recv.at[part, step])
            fixed = {a: own_at[a] for a in order[:step + 1]}
            free = [a for a in AXES if a not in fixed]

            def add(t, carry):
                spots = {}
                rest = t
                for a in reversed(free):
                    spots[a] = lax.rem(rest, 4)
                    rest = rest // 4
                mine = block([fixed[a] if a in fixed else spots[a] for a in AXES], part)
                total = mine[...]
                for d in range(3):
                    total = total + buffer[(d, *[spots[a] for a in free])]
                if step == 2:
                    fin[pl.ds(row, rows), pl.ds(lane, lanes)] = total
                else:
                    mine[...] = total
                return carry

            if free:
                lax.fori_loop(0, 4 ** len(free), add, 0, unroll=4)
            else:
                add(0, 0)
            if step < 2:
                for d in (2, 1, 3):
                    hand_on(part, step + 1, d, fixed)

    fin[...] = fin[...] / den[...]
    for i in range(VS // NZ):
        out[pl.ds(i, 32, stride=VS // NZ), :] = fin[:, i * VS:i * VS + VS]

    for k in range(nk):
        settle(abuf[k].at[pl.ds(0, 31)], a_send)
        settle(bbuf[k].at[pl.ds(0, 3), pl.ds(0, CHUNKS[k][1] // 8)], b_send)
    for n in range(NZ):
        merges[n].wait_send()
    for part in range(3):
        for step in range(3):
            settle(q[3 * part + step], q_send.at[part, step])


def contract(amps, ints, irrep, occ, virt):
    nk = len(CHUNKS)
    dma = pltpu.SemaphoreType.DMA
    widest = max(size for _, size in CHUNKS)
    scratch = [pltpu.VMEM((OCC, 32, size), BF16) for _, size in CHUNKS]
    scratch += [pltpu.VMEM((NZ, size // 8 + 2 * MARGIN, 8, 256), BF16) for _, size in CHUNKS]
    scratch += [
        pltpu.VMEM((1024, widest), BF16),
        pltpu.VMEM((widest, 1024), BF16),
        pltpu.VMEM((widest, 1024), BF16),
        pltpu.VMEM((1024, 1024), BF16),
        pltpu.VMEM((1024, 1024), BF16),
        pltpu.VMEM((8, 512), F32),
        pltpu.VMEM((LANES, 128), I32),
        pltpu.VMEM((8, 1024), I32),
        pltpu.VMEM((32, 256), F32),
        pltpu.VMEM((32, 256), F32),
        pltpu.VMEM((NZ, 4, 4, 2, 32, 256), F32),
        pltpu.VMEM((NZ, 4, 4, 32, 256), F32),
        pltpu.VMEM((1, V), I32),
        pltpu.SMEM((1, OCC), F32),
        pltpu.SMEM((1, VS), F32),
    ]
    for _, rows, _, lanes, _ in PARTS:
        for dims in STEP_DIMS:
            scratch.append(pltpu.VMEM((3, *dims, rows, lanes), F32))
    scratch += [
        dma, dma, dma((nk,)), dma((nk,)), dma((nk, 2)), dma((3,)), dma((NZ,)), dma((NZ,)),
        dma((3, 3)), dma((3, 3)),
    ]
    return pl.pallas_call(
        kernel,
        out_shape=jax.ShapeDtypeStruct((OCC * VS // NZ, VS), F32),
        in_specs=[pl.BlockSpec(memory_space=pltpu.HBM)] * 5,
        out_specs=pl.BlockSpec(memory_space=pltpu.VMEM),
        scratch_shapes=scratch,
        compiler_params=pltpu.CompilerParams(
            collective_id=0, has_side_effects=True, vmem_limit_bytes=64 << 20
        ),
    )(amps, ints, irrep, occ, virt)


def local(amplitudes, integrals, virt_irrep, occ_energy, slab_energy):
    update = contract(
        amplitudes.reshape(OCC, V * V), integrals.reshape(GROUPS, 8, 256),
        virt_irrep.reshape(1, V), occ_energy.reshape(1, OCC), slab_energy.reshape(1, VS),
    )
    return update.reshape(1, OCC, VS // NZ, VS)


def solution(mesh):
    placed = (P("pair", None, None), P("pair", "slab"), P(), P(), P())
    return jax.shard_map(
        local, mesh=mesh, in_specs=placed, out_specs=P("pair", None, "slab", None), check_vma=False
    )
```

```python
import jax
import jax.numpy as jnp
from jax import lax
from jax.experimental import pallas as pl
from jax.experimental.pallas import tpu as pltpu
from jax.sharding import PartitionSpec as P

F32, BF16, I32 = jnp.float32, jnp.bfloat16, jnp.int32
V, VS, OCC = 400, 32, 32
NZ = 4
ROWS = 5000
GROUPS = ROWS // 8
LANES = 1280
SIZE = 256
NK = LANES // SIZE
MARGIN = 16
PARTS = (
    (0, 24, 0, 128, ("z", "x", "y")),
    (0, 24, 128, 128, ("x", "y", "z")),
    (24, 8, 0, 256, ("y", "z", "x")),
)
STEP_DIMS = ((4, 4), (4,), ())
AXES = ("z", "x", "y")


def shift(i, d, n):
    return lax.rem(i + d, n)


def remote(src, dst, send, recv, pair, slab):
    return pltpu.make_async_remote_copy(
        src_ref=src, dst_ref=dst, send_sem=send, recv_sem=recv,
        device_id={"pair": pair, "slab": slab}, device_id_type=pl.DeviceIdType.MESH,
    )


def settle(ref, sem):
    pltpu.make_async_copy(ref, ref, sem).wait()


def one_hot(test):
    return jnp.where(test, F32(1), F32(0)).astype(BF16)


def kernel(amps, ints, irrep, occ, virt, out, *refs):
    abuf, sib, bbuf, bm, bp = refs[:5]
    refs = refs[5:]
    ap, perm_own, perm_sib, perm_ab, vrow, rowirr, colirr, den, fin, c_ref = refs[:10]
    irrep_v, occ_s, virt_s = refs[10:13]
    q, via = refs[13:22], refs[22:25]
    a_send, b_send, x_send, a_recv, b_recv, x_recv, own_sem, arg_sem, v_send, v_recv, q_send, q_recv = (
        refs[25:]
    )

    p = lax.axis_index("pair")
    s = lax.axis_index("slab")
    x, y, c = p // 8, lax.rem(p // 2, 4), lax.rem(p, 2)
    place = {"z": s, "x": x, "y": y}
    chip = p // 2
    sibling = p + 1 - 2 * c

    def chip_at(dx, dy):
        return shift(x, dx, 4) * 4 + shift(y, dy, 4)

    barrier = pltpu.get_barrier_semaphore()

    def greet(pair, slab):
        pl.semaphore_signal(
            barrier, inc=1, device_id={"pair": pair, "slab": slab},
            device_id_type=pl.DeviceIdType.MESH,
        )

    def greet_some(dy, carry):
        for dx in (2, 1, 3, 0):
            greet(chip_at(dx, dy + dx) * 2 + c, s)
        return carry

    for dx in (2, 1, 3):
        greet(chip_at(dx, dx) * 2 + c, s)
    lax.fori_loop(1, 4, greet_some, 0)
    for dz in (2, 1, 3):
        greet(p, shift(s, dz, NZ))
    greet(sibling, s)
    small = [
        pltpu.make_async_copy(src, dst, arg_sem.at[i])
        for i, (src, dst) in enumerate(((irrep, irrep_v), (occ, occ_s), (virt, virt_s)))
    ]
    for copy in small:
        copy.start()
    pl.semaphore_wait(barrier, 19)

    first_tile = ROWS * p // 128
    lead = lax.rem(p, 16)

    def columns(pair, k):
        tile = ROWS * pair // 128 + 10 * s
        return pl.ds(pl.multiple_of(tile * 128 + k * SIZE, 128), SIZE)

    def rows_for(slab, k):
        want = 160 * slab - lead + k * (SIZE // 8)
        have = jnp.clip(want, 0, GROUPS - SIZE // 8)
        return pl.ds(have, SIZE // 8), pl.ds(MARGIN + have - want, SIZE // 8)

    def own_copies(k):
        source, target = rows_for(s, k)
        return [
            pltpu.make_async_copy(ints.at[source], bbuf.at[k, 3, target], own_sem.at[k, 2]),
        ] + [
            pltpu.make_async_copy(
                amps.at[:, columns(chip * 2 + w, k)], abuf.at[k, w, chip], own_sem.at[k, w]
            )
            for w in range(2)
        ]

    def send_amps(k, dx, dy, w):
        peer = chip_at(dx, dy) * 2
        remote(
            amps.at[:, columns(peer + w, k)], abuf.at[k, w, chip], a_send, a_recv.at[k], peer + c, s
        ).start()

    def send_chunk(k, carry):
        for dz in (1, 3, 2):
            slab = shift(s, dz, NZ)
            source, target = rows_for(slab, k)
            remote(
                ints.at[source], bbuf.at[k, 3 - dz, target], b_send, b_recv.at[k], p, slab
            ).start()
        for w in range(2):
            for dx in (1, 3, 2):
                send_amps(k, dx, dx, w)

        def send_some(i, carry):
            for dx in (1, 3, 2, 0):
                send_amps(k, dx, i // 2 + dx, lax.rem(i, 2))
            return carry

        lax.fori_loop(2, 8, send_some, 0)
        for copy in own_copies(k):
            copy.start()
        return carry

    lax.fori_loop(0, NK, send_chunk, 0)

    def orbitals(col):
        return ((((col >> 8) + s + 1) & 3) << 3) | ((col >> 5) & 7), col & 31

    def fill_perm(t, carry):
        row = lax.broadcasted_iota(I32, (128, 1024), 0) + t * 128
        col = lax.broadcasted_iota(I32, (128, 1024), 1)
        rows = pl.ds(pl.multiple_of(t * 128, 128), 128)
        a, b = orbitals(col)
        perm_ab[rows, :] = one_hot(
            row == (((((b >> 3) + 3 - s) & 3) << 8) | ((b & 7) << 5) | a)
        )
        return carry

    lax.fori_loop(0, 8, fill_perm, 0)

    def fill_swap(t, carry):
        row = lax.broadcasted_iota(I32, (128, 512), 0) + t * 128
        col = lax.broadcasted_iota(I32, (128, 512), 1)
        rows = pl.ds(pl.multiple_of(t * 128, 128), 128)
        i, j = ((row >> 5) << 1) + c, row & 31
        here = (((j >> 1) << 5) | i) == col
        perm_own[rows, :] = one_hot(here & ((j & 1) == c))
        perm_sib[rows, :] = one_hot(here & ((j & 1) != c))
        return carry

    lax.fori_loop(0, 4, fill_swap, 0)
    for copy in small:
        copy.wait()

    vrow[...] = jnp.zeros_like(vrow)
    vrow[0:1, 0:V] = irrep_v[...].astype(F32)
    table = jnp.broadcast_to(vrow[0:1, :], (128, 512)).astype(BF16)

    def look_up(lhs, rhs, dims):
        return lax.dot_general(
            lhs, rhs, (dims, ((), ())), preferred_element_type=F32
        ).astype(I32)

    orb = lax.broadcasted_iota(I32, (128, 1024), 0)
    col = lax.broadcasted_iota(I32, (128, 1024), 1)
    first = table[0:16, 0:128]
    of_a, of_b = (look_up(first, one_hot(orb == v), ((1,), (0,))) for v in orbitals(col))
    colirr[...] = (of_a ^ of_b)[0:8]

    start = (first_tile + 10 * s) * 128

    def fill_rows(t, carry):
        base = start + t * 256
        c0 = base // V
        row = lax.broadcasted_iota(I32, (256, 512), 0) + base
        orb = lax.broadcasted_iota(I32, (256, 512), 1)
        cc = jnp.where(row >= (c0 + 1) * V, c0 + 1, c0)
        of_c = look_up(one_hot(orb == cc), table, ((1,), (1,)))
        of_d = look_up(one_hot(orb == row - cc * V), table, ((1,), (1,)))
        row = row[:, 0:128]
        inside = (row >= ROWS * p) & (row < ROWS * p + ROWS)
        rowirr[pl.ds(pl.multiple_of(t * 256, 256), 256), :] = jnp.where(inside, of_c ^ of_d, -1)
        return carry

    lax.fori_loop(0, LANES // 256, fill_rows, 0)

    lane = lax.broadcasted_iota(I32, (8, 256), 1)
    row = lax.broadcasted_iota(I32, (32, 256), 0)
    of_a = jnp.zeros((8, 256), F32)
    of_b = jnp.zeros((8, 256), F32)
    of_j = jnp.zeros((32, 256), F32)
    for i in range(VS // NZ):
        of_a = jnp.where((lane >> 5) == i, virt_s[0, s * (VS // NZ) + i], of_a)
    for i in range(VS):
        of_b = jnp.where((lane & 31) == i, virt_s[0, i], of_b)
    for i in range(OCC):
        of_j = jnp.where(row == i, occ_s[0, i], of_j)
    den[...] = ((of_a + of_b) - occ_s[0, p])[0:1] - of_j

    own_at = {"z": 3, "x": x, "y": y}

    def block(index, part):
        row, rows, lane, lanes, _ = PARTS[part]
        return c_ref.at[(*index, pl.ds(row, rows), pl.ds(lane, lanes))]

    def peer_at(axis, d):
        at = {**place, axis: shift(place[axis], d, 4)}
        return at["x"] * 8 + at["y"] * 2 + c, at["z"]

    def share(axis, d):
        return d - 1 if axis == "z" else shift(place[axis], d, 4)

    def half(part, d, h):
        axis = PARTS[part][4][0]
        index = [share(axis, d) if a == axis else slice(None) for a in AXES]
        index[1 if axis == "z" else 0] = pl.ds(2 * h, 2)
        return block(index, part)

    def halfway(part, h):
        remote(
            half(part, 2, h), via[part].at[h], v_send.at[part], v_recv.at[part, h],
            *peer_at(PARTS[part][4][0], 3 if h else 1),
        ).start()

    def pass_on(part, d, h):
        remote(
            half(part, d, h), q[3 * part].at[0 if d == 1 else 1, pl.ds(2 * h, 2)],
            q_send.at[part, 0], q_recv.at[part, 0], *peer_at(PARTS[part][4][0], d),
        ).start()

    def begin(part):
        halfway(part, 0)
        halfway(part, 1)

    def straight(part):
        pass_on(part, 1, 1)
        pass_on(part, 3, 0)

    def hand_on(part, step, d, fixed):
        axis = PARTS[part][4][step]
        fixed = {**fixed, axis: share(axis, d)}
        remote(
            block([fixed.get(a, slice(None)) for a in AXES], part), q[3 * part + step].at[d - 1],
            q_send.at[part, step], q_recv.at[part, step], *peer_at(axis, d),
        ).start()

    def swap(src, dst, k, kind):
        return remote(src, dst, x_send.at[k, kind], x_recv.at[k, kind], sibling, s)

    def swap_ints(k):
        return swap(bm.at[k, c], bm.at[k, c], k, 0)

    def swap_amps(k):
        return swap(abuf.at[k], sib.at[k], k, 1)

    def clear(n, carry):
        c_ref[n] = jnp.zeros((4, 4, 32, 256), F32)
        return carry

    lax.fori_loop(0, NZ, clear, 0)

    def contract_chunk(k, carry):
        settle(abuf.at[k, :, pl.ds(0, 15)], a_recv.at[k])
        for copy in own_copies(k):
            copy.wait()
        swap_amps(k).start()
        settle(bbuf.at[k, pl.ds(0, 3), pl.ds(0, SIZE // 8)], b_recv.at[k])

        def mask(t, carry):
            rows = pl.multiple_of(t * 128, 128)
            row_irrep = rowirr[pl.ds(pl.multiple_of(k * SIZE + rows, 128), 128), :]
            for block in range(8):
                n, side = block // 2, block % 2
                part = bbuf[k, n, pl.ds(MARGIN + t * 16, 16), :, pl.ds(side * 128, 128)]
                part = part.astype(F32).reshape(128, 128)
                keep = row_irrep == colirr[0:1, block * 128:block * 128 + 128]
                bm[k, c, pl.ds(rows, 128), block * 128:block * 128 + 128] = jnp.where(
                    keep, part, F32(0)
                ).astype(BF16)
            return carry

        lax.fori_loop(0, SIZE // 128, mask, 0)
        swap_ints(k).start()

        def transpose(w):
            bp[w] = jnp.dot(bm[k, w], perm_ab[...], preferred_element_type=F32).astype(BF16)

        transpose(c)
        swap_amps(k).wait_recv()

        for w in range(2):
            mirrored = jnp.dot(
                perm_own[...], abuf[k, w].reshape(512, SIZE), preferred_element_type=F32
            ) + jnp.dot(perm_sib[...], sib[k, w].reshape(512, SIZE), preferred_element_type=F32)
            ap[w] = mirrored.astype(BF16)
        swap_ints(k).wait_recv()
        transpose(1 - c)
        for n in (1, 0, 2, 3):
            cols = slice(n * 256, n * 256 + 256)
            total = None
            for w in range(2):
                for left, right in (
                    (abuf[k, w].reshape(512, SIZE), bm[k, w, :, cols]), (ap[w], bp[w, :, cols])
                ):
                    term = jnp.dot(left, right, preferred_element_type=F32)
                    total = term if total is None else total + term
            c_ref[n] += total.reshape(4, 4, 32, 256)

            @pl.when(k == NK - 1)
            def _():
                if n == 1:
                    begin(0)
                elif n == 0:
                    halfway(1, 0)
                    halfway(2, 0)
                elif n == 2:
                    straight(0)
                else:
                    halfway(1, 1)
                    halfway(2, 1)
                    straight(1)
                    straight(2)

        return carry

    lax.fori_loop(0, NK, contract_chunk, 0)
    for part in range(3):
        for h, d in ((0, 1), (1, 3)):
            settle(via[part].at[h], v_recv.at[part, h])
            mine = half(part, d, h)

            def join(t, carry):
                i, j = t // 4, lax.rem(t, 4)
                mine[i, j] = mine[i, j] + via[part][h, i, j]
                return carry

            lax.fori_loop(0, 8, join, 0, unroll=2)
            pass_on(part, d, h)

    for step in range(3):
        for part, (row, rows, lane, lanes, order) in enumerate(PARTS):
            buffer = q[3 * part + step]
            settle(buffer, q_recv.at[part, step])
            fixed = {a: own_at[a] for a in order[:step + 1]}
            mine = block([fixed.get(a, slice(None)) for a in AXES], part)
            if step == 0:
                def add(t, carry):
                    i, j = t // 4, lax.rem(t, 4)
                    mine[i, j] = mine[i, j] + buffer[0, i, j] + buffer[1, i, j]
                    return carry

                lax.fori_loop(0, 16, add, 0, unroll=2)
            else:
                total = ((mine[...] + buffer[0]) + buffer[1]) + buffer[2]
                if step == 2:
                    fin[pl.ds(row, rows), pl.ds(lane, lanes)] = total
                    continue
                mine[...] = total
            for d in (2, 1, 3):
                hand_on(part, step + 1, d, fixed)

    fin[...] = fin[...] / den[...]
    for i in range(VS // NZ):
        out[pl.ds(i, 32, stride=VS // NZ), :] = fin[:, i * VS:i * VS + VS]

    def drain(k, carry):
        settle(abuf.at[k, :, pl.ds(0, 15)], a_send)
        settle(bbuf.at[k, pl.ds(0, 3), pl.ds(0, SIZE // 8)], b_send)
        swap_ints(k).wait_send()
        swap_amps(k).wait_send()
        return carry

    lax.fori_loop(0, NK, drain, 0)
    for part in range(3):
        for step in range(3):
            settle(q[3 * part + step], q_send.at[part, step])
        settle(via[part], v_send.at[part])


def contract(amps, ints, irrep, occ, virt):
    dma = pltpu.SemaphoreType.DMA
    scratch = [
        pltpu.VMEM((NK, 2, 16, 32, SIZE), BF16),
        pltpu.VMEM((NK, 2, 16, 32, SIZE), BF16),
        pltpu.VMEM((NK, NZ, SIZE // 8 + 2 * MARGIN, 8, 256), BF16),
        pltpu.VMEM((NK, 2, SIZE, 1024), BF16),
        pltpu.VMEM((2, SIZE, 1024), BF16),
        pltpu.VMEM((2, 512, SIZE), BF16),
        pltpu.VMEM((512, 512), BF16),
        pltpu.VMEM((512, 512), BF16),
        pltpu.VMEM((1024, 1024), BF16),
        pltpu.VMEM((8, 512), F32),
        pltpu.VMEM((LANES, 128), I32),
        pltpu.VMEM((8, 1024), I32),
        pltpu.VMEM((32, 256), F32),
        pltpu.VMEM((32, 256), F32),
        pltpu.VMEM((NZ, 4, 4, 32, 256), F32),
        pltpu.VMEM((1, V), I32),
        pltpu.SMEM((1, OCC), F32),
        pltpu.SMEM((1, VS), F32),
    ]
    for _, rows, _, lanes, _ in PARTS:
        for step, dims in enumerate(STEP_DIMS):
            scratch.append(pltpu.VMEM((3 if step else 2, *dims, rows, lanes), F32))
    scratch += [pltpu.VMEM((2, 2, 4, rows, lanes), F32) for _, rows, _, lanes, _ in PARTS]
    scratch += [
        dma, dma, dma((NK, 2)), dma((NK,)), dma((NK,)), dma((NK, 2)), dma((NK, 3)), dma((3,)),
        dma((3,)), dma((3, 2)), dma((3, 3)), dma((3, 3)),
    ]
    return pl.pallas_call(
        kernel,
        out_shape=jax.ShapeDtypeStruct((OCC * VS // NZ, VS), F32),
        in_specs=[pl.BlockSpec(memory_space=pltpu.HBM)] * 5,
        out_specs=pl.BlockSpec(memory_space=pltpu.VMEM),
        scratch_shapes=scratch,
        compiler_params=pltpu.CompilerParams(
            collective_id=0, has_side_effects=True, vmem_limit_bytes=64 << 20
        ),
    )(amps, ints, irrep, occ, virt)


def local(amplitudes, integrals, virt_irrep, occ_energy, slab_energy):
    update = contract(
        amplitudes.reshape(OCC, V * V), integrals.reshape(GROUPS, 8, 256),
        virt_irrep.reshape(1, V), occ_energy.reshape(1, OCC), slab_energy.reshape(1, VS),
    )
    return update.reshape(1, OCC, VS // NZ, VS)


def solution(mesh):
    placed = (P("pair", None, None), P("pair", "slab"), P(), P(), P())
    return jax.shard_map(
        local, mesh=mesh, in_specs=placed, out_specs=P("pair", None, "slab", None), check_vma=False
    )
```

```python
import jax
import jax.numpy as jnp
from jax import lax
from jax.experimental import pallas as pl
from jax.experimental.pallas import tpu as pltpu
from jax.sharding import PartitionSpec as P

F32, BF16, I32 = jnp.float32, jnp.bfloat16, jnp.int32
V, VS, OCC = 400, 32, 32
NZ = 4
ROWS = 5000
GROUPS = ROWS // 8
LANES = 1280
SIZE = 256
NK = LANES // SIZE
MARGIN = 16
PARTS = (
    (0, 24, 0, 128, ("z", "x", "y")),
    (0, 24, 128, 128, ("x", "y", "z")),
    (24, 8, 0, 256, ("y", "z", "x")),
)
STEP_DIMS = ((4, 4), (4,), ())


def shift(i, d, n):
    return lax.rem(i + d, n)


def remote(src, dst, send, recv, pair, slab):
    return pltpu.make_async_remote_copy(
        src_ref=src, dst_ref=dst, send_sem=send, recv_sem=recv,
        device_id={"pair": pair, "slab": slab}, device_id_type=pl.DeviceIdType.MESH,
    )


def settle(ref, sem):
    pltpu.make_async_copy(ref, ref, sem).wait()


def one_hot(test):
    return jnp.where(test, F32(1), F32(0)).astype(BF16)


def kernel(amps, ints, irrep, occ, virt, out, *refs):
    abuf, sib, bbuf, bm, bp = refs[:5]
    refs = refs[5:]
    ap, perm_own, perm_sib, perm_ab, vrow, rowirr, colirr, den, fin = refs[:9]
    sums, refs = refs[9:12], refs[12:]
    irrep_v, occ_s, virt_s = refs[:3]
    q, via = refs[3:12], refs[12:15]
    a_send, b_send, x_send, a_recv, b_recv, x_recv, own_sem, arg_sem, v_send, v_recv, q_send, q_recv = (
        refs[15:]
    )

    p = lax.axis_index("pair")
    s = lax.axis_index("slab")
    x, y, c = p // 8, lax.rem(p // 2, 4), lax.rem(p, 2)
    place = {"z": s, "x": x, "y": y}
    chip = p // 2
    sibling = p + 1 - 2 * c

    def chip_at(dx, dy):
        return shift(x, dx, 4) * 4 + shift(y, dy, 4)

    barrier = pltpu.get_barrier_semaphore()

    def greet(pair, slab):
        pl.semaphore_signal(
            barrier, inc=1, device_id={"pair": pair, "slab": slab},
            device_id_type=pl.DeviceIdType.MESH,
        )

    def greet_some(dy, carry):
        for dx in (2, 1, 3, 0):
            greet(chip_at(dx, dy + dx) * 2 + c, s)
        return carry

    for dx in (2, 1, 3):
        greet(chip_at(dx, dx) * 2 + c, s)
    lax.fori_loop(1, 4, greet_some, 0)
    for dz in (2, 1, 3):
        greet(p, shift(s, dz, NZ))
    greet(sibling, s)
    small = [
        pltpu.make_async_copy(src, dst, arg_sem.at[i])
        for i, (src, dst) in enumerate(((irrep, irrep_v), (occ, occ_s), (virt, virt_s)))
    ]
    for copy in small:
        copy.start()
    pl.semaphore_wait(barrier, 19)

    first_tile = ROWS * p // 128
    lead = lax.rem(p, 16)

    def columns(pair, k):
        tile = ROWS * pair // 128 + 10 * s
        return pl.ds(pl.multiple_of(tile * 128 + k * SIZE, 128), SIZE)

    def rows_for(slab, k):
        want = 160 * slab - lead + k * (SIZE // 8)
        have = jnp.clip(want, 0, GROUPS - SIZE // 8)
        return pl.ds(have, SIZE // 8), pl.ds(MARGIN + have - want, SIZE // 8)

    def own_copies(k):
        source, target = rows_for(s, k)
        return [
            pltpu.make_async_copy(ints.at[source], bbuf.at[k, 3, target], own_sem.at[k, 2]),
        ] + [
            pltpu.make_async_copy(
                amps.at[:, columns(chip * 2 + w, k)], abuf.at[k, w, chip], own_sem.at[k, w]
            )
            for w in range(2)
        ]

    def send_amps(k, dx, dy, w):
        peer = chip_at(dx, dy) * 2
        remote(
            amps.at[:, columns(peer + w, k)], abuf.at[k, w, chip], a_send, a_recv.at[k], peer + c, s
        ).start()

    def send_chunk(k, carry):
        for dz in (1, 3, 2):
            slab = shift(s, dz, NZ)
            source, target = rows_for(slab, k)
            remote(
                ints.at[source], bbuf.at[k, 3 - dz, target], b_send, b_recv.at[k], p, slab
            ).start()
        for w in range(2):
            for dx in (1, 3, 2):
                send_amps(k, dx, dx, w)

        def send_some(i, carry):
            for dx in (1, 3, 2, 0):
                send_amps(k, dx, i // 2 + dx, lax.rem(i, 2))
            return carry

        lax.fori_loop(2, 8, send_some, 0)
        for copy in own_copies(k):
            copy.start()
        return carry

    lax.fori_loop(0, NK, send_chunk, 0)

    def orbitals(col):
        return ((((col >> 8) + s + 1) & 3) << 3) | ((col >> 5) & 7), col & 31

    def fill_perm(t, carry):
        row = lax.broadcasted_iota(I32, (128, 1024), 0) + t * 128
        col = lax.broadcasted_iota(I32, (128, 1024), 1)
        rows = pl.ds(pl.multiple_of(t * 128, 128), 128)
        a, b = orbitals(col)
        perm_ab[rows, :] = one_hot(
            row == (((((b >> 3) + 3 - s) & 3) << 8) | ((b & 7) << 5) | a)
        )
        return carry

    lax.fori_loop(0, 8, fill_perm, 0)

    def fill_swap(t, carry):
        row = lax.broadcasted_iota(I32, (128, 512), 0) + t * 128
        col = lax.broadcasted_iota(I32, (128, 512), 1)
        rows = pl.ds(pl.multiple_of(t * 128, 128), 128)
        i, j = ((row >> 5) << 1) + c, row & 31
        here = (((j >> 1) << 5) | i) == col
        perm_own[rows, :] = one_hot(here & ((j & 1) == c))
        perm_sib[rows, :] = one_hot(here & ((j & 1) != c))
        return carry

    lax.fori_loop(0, 4, fill_swap, 0)
    for copy in small:
        copy.wait()

    vrow[...] = jnp.zeros_like(vrow)
    vrow[0:1, 0:V] = irrep_v[...].astype(F32)
    table = jnp.broadcast_to(vrow[0:1, :], (128, 512)).astype(BF16)

    def look_up(lhs, rhs, dims):
        return lax.dot_general(
            lhs, rhs, (dims, ((), ())), preferred_element_type=F32
        ).astype(I32)

    orb = lax.broadcasted_iota(I32, (128, 1024), 0)
    col = lax.broadcasted_iota(I32, (128, 1024), 1)
    first = table[0:16, 0:128]
    of_a, of_b = (look_up(first, one_hot(orb == v), ((1,), (0,))) for v in orbitals(col))
    colirr[...] = (of_a ^ of_b)[0:8]

    start = (first_tile + 10 * s) * 128

    def fill_rows(t, carry):
        base = start + t * 256
        c0 = base // V
        row = lax.broadcasted_iota(I32, (256, 512), 0) + base
        orb = lax.broadcasted_iota(I32, (256, 512), 1)
        cc = jnp.where(row >= (c0 + 1) * V, c0 + 1, c0)
        of_c = look_up(one_hot(orb == cc), table, ((1,), (1,)))
        of_d = look_up(one_hot(orb == row - cc * V), table, ((1,), (1,)))
        row = row[:, 0:128]
        inside = (row >= ROWS * p) & (row < ROWS * p + ROWS)
        rowirr[pl.ds(pl.multiple_of(t * 256, 256), 256), :] = jnp.where(inside, of_c ^ of_d, -1)
        return carry

    lax.fori_loop(0, LANES // 256, fill_rows, 0)

    lane = lax.broadcasted_iota(I32, (8, 256), 1)
    row = lax.broadcasted_iota(I32, (32, 256), 0)
    of_a = jnp.zeros((8, 256), F32)
    of_b = jnp.zeros((8, 256), F32)
    of_j = jnp.zeros((32, 256), F32)
    for i in range(VS // NZ):
        of_a = jnp.where((lane >> 5) == i, virt_s[0, s * (VS // NZ) + i], of_a)
    for i in range(VS):
        of_b = jnp.where((lane & 31) == i, virt_s[0, i], of_b)
    for i in range(OCC):
        of_j = jnp.where(row == i, occ_s[0, i], of_j)
    den[...] = ((of_a + of_b) - occ_s[0, p])[0:1] - of_j

    own_at = {"z": 3, "x": x, "y": y}

    def peer_at(axis, d):
        at = {**place, axis: shift(place[axis], d, 4)}
        return at["x"] * 8 + at["y"] * 2 + c, at["z"]

    def share(axis, d):
        return d - 1 if axis == "z" else shift(place[axis], d, 4)

    def half(part, d, h):
        return sums[part].at[share(PARTS[part][4][0], d), pl.ds(2 * h, 2)]

    def halfway(part, h):
        remote(
            half(part, 2, h), via[part].at[h], v_send.at[part], v_recv.at[part, h],
            *peer_at(PARTS[part][4][0], 3 if h else 1),
        ).start()

    def pass_on(part, d, h):
        remote(
            half(part, d, h), q[3 * part].at[0 if d == 1 else 1, pl.ds(2 * h, 2)],
            q_send.at[part, 0], q_recv.at[part, 0], *peer_at(PARTS[part][4][0], d),
        ).start()

    def begin(part):
        halfway(part, 0)
        halfway(part, 1)

    def straight(part):
        pass_on(part, 1, 1)
        pass_on(part, 3, 0)

    def hand_on(part, step, d):
        order = PARTS[part][4]
        remote(
            sums[part].at[(*[own_at[a] for a in order[:step]], share(order[step], d))],
            q[3 * part + step].at[d - 1],
            q_send.at[part, step], q_recv.at[part, step], *peer_at(order[step], d),
        ).start()

    def swap(src, dst, k, kind):
        return remote(src, dst, x_send.at[k, kind], x_recv.at[k, kind], sibling, s)

    def swap_ints(k):
        return swap(bm.at[k, c], bm.at[k, c], k, 0)

    def swap_amps(k):
        return swap(abuf.at[k], sib.at[k], k, 1)

    def clear(n, carry):
        for part in sums:
            part[n] = jnp.zeros(part.shape[1:], F32)
        return carry

    lax.fori_loop(0, 4, clear, 0)

    def contract_chunk(k, carry):
        settle(bbuf.at[k, pl.ds(0, 3), pl.ds(0, SIZE // 8)], b_recv.at[k])
        own_copies(k)[0].wait()

        def mask(t, carry):
            rows = pl.multiple_of(t * 128, 128)
            row_irrep = rowirr[pl.ds(pl.multiple_of(k * SIZE + rows, 128), 128), :]
            for block in range(8):
                n, side = block // 2, block % 2
                part = bbuf[k, n, pl.ds(MARGIN + t * 16, 16), :, pl.ds(side * 128, 128)]
                part = part.astype(F32).reshape(128, 128)
                keep = row_irrep == colirr[0:1, block * 128:block * 128 + 128]
                bm[k, c, pl.ds(rows, 128), block * 128:block * 128 + 128] = jnp.where(
                    keep, part, F32(0)
                ).astype(BF16)
            return carry

        lax.fori_loop(0, SIZE // 128, mask, 0)
        swap_ints(k).start()

        def transpose(w):
            bp[w] = jnp.dot(bm[k, w], perm_ab[...], preferred_element_type=F32).astype(BF16)

        transpose(c)
        settle(abuf.at[k, :, pl.ds(0, 15)], a_recv.at[k])
        for copy in own_copies(k)[1:]:
            copy.wait()
        swap_amps(k).start()
        swap_ints(k).wait_recv()
        transpose(1 - c)
        swap_amps(k).wait_recv()

        for w in range(2):
            mirrored = jnp.dot(
                perm_own[...], abuf[k, w].reshape(512, SIZE), preferred_element_type=F32
            ) + jnp.dot(perm_sib[...], sib[k, w].reshape(512, SIZE), preferred_element_type=F32)
            ap[w] = mirrored.astype(BF16)
        for n in range(NZ):
            cols = slice(n * 256, n * 256 + 256)
            total = None
            for w in range(2):
                for left, right in (
                    (abuf[k, w].reshape(512, SIZE), bm[k, w, :, cols]), (ap[w], bp[w, :, cols])
                ):
                    term = jnp.dot(left, right, preferred_element_type=F32)
                    total = term if total is None else total + term
            total = total.reshape(4, 4, 32, 256)
            for part, (row, rows, lane, lanes, order) in zip(sums, PARTS):
                for i in range(4):
                    for j in range(4):
                        at = {"z": n, "x": i, "y": j}
                        part[tuple(at[a] for a in order)] += total[
                            i, j, row:row + rows, lane:lane + lanes
                        ]
        return carry

    lax.fori_loop(0, NK, contract_chunk, 0)
    begin(0)
    for h in range(2):
        halfway(1, h)
        halfway(2, h)
    for part in range(3):
        straight(part)
    for part in range(3):
        for h, d in ((0, 1), (1, 3)):
            settle(via[part].at[h], v_recv.at[part, h])
            mine = half(part, d, h)

            mine[...] = mine[...] + via[part][h]
            pass_on(part, d, h)

    for step in range(3):
        for part, (row, rows, lane, lanes, order) in enumerate(PARTS):
            buffer = q[3 * part + step]
            settle(buffer, q_recv.at[part, step])
            mine = sums[part].at[tuple(own_at[a] for a in order[:step + 1])]
            total = mine[...]
            for d in range(3 if step else 2):
                total = total + buffer[d]
            if step == 2:
                fin[pl.ds(row, rows), pl.ds(lane, lanes)] = total
                continue
            mine[...] = total
            for d in (2, 1, 3):
                hand_on(part, step + 1, d)

    fin[...] = fin[...] / den[...]
    for i in range(VS // NZ):
        out[pl.ds(i, 32, stride=VS // NZ), :] = fin[:, i * VS:i * VS + VS]

    def drain(k, carry):
        settle(abuf.at[k, :, pl.ds(0, 15)], a_send)
        settle(bbuf.at[k, pl.ds(0, 3), pl.ds(0, SIZE // 8)], b_send)
        swap_ints(k).wait_send()
        swap_amps(k).wait_send()
        return carry

    lax.fori_loop(0, NK, drain, 0)
    for part in range(3):
        for step in range(3):
            settle(q[3 * part + step], q_send.at[part, step])
        settle(via[part], v_send.at[part])


def contract(amps, ints, irrep, occ, virt):
    dma = pltpu.SemaphoreType.DMA
    scratch = [
        pltpu.VMEM((NK, 2, 16, 32, SIZE), BF16),
        pltpu.VMEM((NK, 2, 16, 32, SIZE), BF16),
        pltpu.VMEM((NK, NZ, SIZE // 8 + 2 * MARGIN, 8, 256), BF16),
        pltpu.VMEM((NK, 2, SIZE, 1024), BF16),
        pltpu.VMEM((2, SIZE, 1024), BF16),
        pltpu.VMEM((2, 512, SIZE), BF16),
        pltpu.VMEM((512, 512), BF16),
        pltpu.VMEM((512, 512), BF16),
        pltpu.VMEM((1024, 1024), BF16),
        pltpu.VMEM((8, 512), F32),
        pltpu.VMEM((LANES, 128), I32),
        pltpu.VMEM((8, 1024), I32),
        pltpu.VMEM((32, 256), F32),
        pltpu.VMEM((32, 256), F32),
        *[pltpu.VMEM((4, 4, 4, rows, lanes), F32) for _, rows, _, lanes, _ in PARTS],
        pltpu.VMEM((1, V), I32),
        pltpu.SMEM((1, OCC), F32),
        pltpu.SMEM((1, VS), F32),
    ]
    for _, rows, _, lanes, _ in PARTS:
        for step, dims in enumerate(STEP_DIMS):
            scratch.append(pltpu.VMEM((3 if step else 2, *dims, rows, lanes), F32))
    scratch += [pltpu.VMEM((2, 2, 4, rows, lanes), F32) for _, rows, _, lanes, _ in PARTS]
    scratch += [
        dma, dma, dma((NK, 2)), dma((NK,)), dma((NK,)), dma((NK, 2)), dma((NK, 3)), dma((3,)),
        dma((3,)), dma((3, 2)), dma((3, 3)), dma((3, 3)),
    ]
    return pl.pallas_call(
        kernel,
        out_shape=jax.ShapeDtypeStruct((OCC * VS // NZ, VS), F32),
        in_specs=[pl.BlockSpec(memory_space=pltpu.HBM)] * 5,
        out_specs=pl.BlockSpec(memory_space=pltpu.VMEM),
        scratch_shapes=scratch,
        compiler_params=pltpu.CompilerParams(
            collective_id=0, has_side_effects=True, vmem_limit_bytes=64 << 20
        ),
    )(amps, ints, irrep, occ, virt)


def local(amplitudes, integrals, virt_irrep, occ_energy, slab_energy):
    update = contract(
        amplitudes.reshape(OCC, V * V), integrals.reshape(GROUPS, 8, 256),
        virt_irrep.reshape(1, V), occ_energy.reshape(1, OCC), slab_energy.reshape(1, VS),
    )
    return update.reshape(1, OCC, VS // NZ, VS)


def solution(mesh):
    placed = (P("pair", None, None), P("pair", "slab"), P(), P(), P())
    return jax.shard_map(
        local, mesh=mesh, in_specs=placed, out_specs=P("pair", None, "slab", None), check_vma=False
    )
```

```python
import jax
import jax.numpy as jnp
from jax import lax
from jax.experimental import pallas as pl
from jax.experimental.pallas import tpu as pltpu
from jax.sharding import PartitionSpec as P

F32, BF16, I32 = jnp.float32, jnp.bfloat16, jnp.int32
V, VS, OCC = 400, 32, 32
NZ = 4
ROWS = 5000
GROUPS = ROWS // 8
LANES = 1280
SIZE = 256
NK = LANES // SIZE
MARGIN = 16
PARTS = (
    (0, 16, 0, 128, ("z", "x", "y")),
    (0, 16, 128, 128, ("x", "y", "z")),
    (24, 8, 0, 256, ("y", "z", "x")),
    (16, 8, 0, 128, ("z", "x", "y")),
    (16, 8, 128, 128, ("x", "y", "z")),
)
NP = len(PARTS)
STEP_DIMS = ((4, 4), (4,), ())


def shift(i, d, n):
    return lax.rem(i + d, n)


def remote(src, dst, send, recv, pair, slab):
    return pltpu.make_async_remote_copy(
        src_ref=src, dst_ref=dst, send_sem=send, recv_sem=recv,
        device_id={"pair": pair, "slab": slab}, device_id_type=pl.DeviceIdType.MESH,
    )


def settle(ref, sem):
    pltpu.make_async_copy(ref, ref, sem).wait()


def one_hot(test):
    return jnp.where(test, F32(1), F32(0)).astype(BF16)


def kernel(amps, ints, irrep, occ, virt, out, *refs):
    abuf, sib, bbuf, bm, bp = refs[:5]
    refs = refs[5:]
    ap, perm_own, perm_sib, perm_ab, vrow, rowirr, colirr, den, fin = refs[:9]
    sums, refs = refs[9:9 + NP], refs[9 + NP:]
    irrep_v, occ_s, virt_s = refs[:3]
    q, via = refs[3:3 + 3 * NP], refs[3 + 3 * NP:3 + 4 * NP]
    a_send, b_send, x_send, a_recv, b_recv, x_recv, own_sem, arg_sem, v_send, v_recv, q_send, q_recv = (
        refs[3 + 4 * NP:]
    )

    p = lax.axis_index("pair")
    s = lax.axis_index("slab")
    x, y, c = p // 8, lax.rem(p // 2, 4), lax.rem(p, 2)
    place = {"z": s, "x": x, "y": y}
    chip = p // 2
    sibling = p + 1 - 2 * c

    def chip_at(dx, dy):
        return shift(x, dx, 4) * 4 + shift(y, dy, 4)

    barrier = pltpu.get_barrier_semaphore()

    def greet(pair, slab):
        pl.semaphore_signal(
            barrier, inc=1, device_id={"pair": pair, "slab": slab},
            device_id_type=pl.DeviceIdType.MESH,
        )

    def greet_some(dy, carry):
        for dx in (2, 1, 3, 0):
            greet(chip_at(dx, dy + dx) * 2 + c, s)
        return carry

    for dx in (2, 1, 3):
        greet(chip_at(dx, dx) * 2 + c, s)
    lax.fori_loop(1, 4, greet_some, 0)
    for dz in (2, 1, 3):
        greet(p, shift(s, dz, NZ))
    greet(sibling, s)
    small = [
        pltpu.make_async_copy(src, dst, arg_sem.at[i])
        for i, (src, dst) in enumerate(((irrep, irrep_v), (occ, occ_s), (virt, virt_s)))
    ]
    for copy in small:
        copy.start()
    pl.semaphore_wait(barrier, 19)

    first_tile = ROWS * p // 128
    lead = lax.rem(p, 16)

    def columns(pair, k):
        tile = ROWS * pair // 128 + 10 * s
        return pl.ds(pl.multiple_of(tile * 128 + k * SIZE, 128), SIZE)

    def rows_for(slab, k):
        want = 160 * slab - lead + k * (SIZE // 8)
        have = jnp.clip(want, 0, GROUPS - SIZE // 8)
        return pl.ds(have, SIZE // 8), pl.ds(MARGIN + have - want, SIZE // 8)

    def own_copies(k):
        source, target = rows_for(s, k)
        return [
            pltpu.make_async_copy(ints.at[source], bbuf.at[k, 3, target], own_sem.at[k, 2]),
        ] + [
            pltpu.make_async_copy(
                amps.at[:, columns(chip * 2 + w, k)], abuf.at[k, w, chip], own_sem.at[k, w]
            )
            for w in range(2)
        ]

    def send_amps(k, dx, dy, w):
        peer = chip_at(dx, dy) * 2
        remote(
            amps.at[:, columns(peer + w, k)], abuf.at[k, w, chip], a_send, a_recv.at[k], peer + c, s
        ).start()

    def send_chunk(k, carry):
        for dz in (1, 3, 2):
            slab = shift(s, dz, NZ)
            source, target = rows_for(slab, k)
            remote(
                ints.at[source], bbuf.at[k, 3 - dz, target], b_send, b_recv.at[k], p, slab
            ).start()
        for w in range(2):
            for dx in (1, 3, 2):
                send_amps(k, dx, dx, w)

        def send_some(i, carry):
            for dx in (1, 3, 2, 0):
                send_amps(k, dx, i // 2 + dx, lax.rem(i, 2))
            return carry

        lax.fori_loop(2, 8, send_some, 0)
        for copy in own_copies(k):
            copy.start()
        return carry

    lax.fori_loop(0, NK, send_chunk, 0)

    def orbitals(col):
        return ((((col >> 8) + s + 1) & 3) << 3) | ((col >> 5) & 7), col & 31

    def fill_perm(t, carry):
        row = lax.broadcasted_iota(I32, (128, 1024), 0) + t * 128
        col = lax.broadcasted_iota(I32, (128, 1024), 1)
        rows = pl.ds(pl.multiple_of(t * 128, 128), 128)
        a, b = orbitals(col)
        perm_ab[rows, :] = one_hot(
            row == (((((b >> 3) + 3 - s) & 3) << 8) | ((b & 7) << 5) | a)
        )
        return carry

    lax.fori_loop(0, 8, fill_perm, 0)

    def fill_swap(t, carry):
        row = lax.broadcasted_iota(I32, (128, 512), 0) + t * 128
        col = lax.broadcasted_iota(I32, (128, 512), 1)
        rows = pl.ds(pl.multiple_of(t * 128, 128), 128)
        i, j = ((row >> 5) << 1) + c, row & 31
        here = (((j >> 1) << 5) | i) == col
        perm_own[rows, :] = one_hot(here & ((j & 1) == c))
        perm_sib[rows, :] = one_hot(here & ((j & 1) != c))
        return carry

    lax.fori_loop(0, 4, fill_swap, 0)
    for copy in small:
        copy.wait()

    vrow[...] = jnp.zeros_like(vrow)
    vrow[0:1, 0:V] = irrep_v[...].astype(F32)
    table = jnp.broadcast_to(vrow[0:1, :], (128, 512)).astype(BF16)

    def look_up(lhs, rhs, dims):
        return lax.dot_general(
            lhs, rhs, (dims, ((), ())), preferred_element_type=F32
        ).astype(I32)

    orb = lax.broadcasted_iota(I32, (128, 1024), 0)
    col = lax.broadcasted_iota(I32, (128, 1024), 1)
    first = table[0:16, 0:128]
    of_a, of_b = (look_up(first, one_hot(orb == v), ((1,), (0,))) for v in orbitals(col))
    colirr[...] = (of_a ^ of_b)[0:8]

    start = (first_tile + 10 * s) * 128

    def fill_rows(t, carry):
        base = start + t * 256
        c0 = base // V
        row = lax.broadcasted_iota(I32, (256, 512), 0) + base
        orb = lax.broadcasted_iota(I32, (256, 512), 1)
        cc = jnp.where(row >= (c0 + 1) * V, c0 + 1, c0)
        of_c = look_up(one_hot(orb == cc), table, ((1,), (1,)))
        of_d = look_up(one_hot(orb == row - cc * V), table, ((1,), (1,)))
        row = row[:, 0:128]
        inside = (row >= ROWS * p) & (row < ROWS * p + ROWS)
        rowirr[pl.ds(pl.multiple_of(t * 256, 256), 256), :] = jnp.where(inside, of_c ^ of_d, -1)
        return carry

    lax.fori_loop(0, LANES // 256, fill_rows, 0)

    lane = lax.broadcasted_iota(I32, (8, 256), 1)
    row = lax.broadcasted_iota(I32, (32, 256), 0)
    of_a = jnp.zeros((8, 256), F32)
    of_b = jnp.zeros((8, 256), F32)
    of_j = jnp.zeros((32, 256), F32)
    for i in range(VS // NZ):
        of_a = jnp.where((lane >> 5) == i, virt_s[0, s * (VS // NZ) + i], of_a)
    for i in range(VS):
        of_b = jnp.where((lane & 31) == i, virt_s[0, i], of_b)
    for i in range(OCC):
        of_j = jnp.where(row == i, occ_s[0, i], of_j)
    den[...] = ((of_a + of_b) - occ_s[0, p])[0:1] - of_j

    own_at = {"z": 3, "x": x, "y": y}

    def peer_at(axis, d):
        at = {**place, axis: shift(place[axis], d, 4)}
        return at["x"] * 8 + at["y"] * 2 + c, at["z"]

    def share(axis, d):
        return d - 1 if axis == "z" else shift(place[axis], d, 4)

    def half(part, d, h):
        return sums[part].at[share(PARTS[part][4][0], d), pl.ds(2 * h, 2)]

    def halfway(part, h):
        remote(
            half(part, 2, h), via[part].at[h], v_send.at[part], v_recv.at[part, h],
            *peer_at(PARTS[part][4][0], 3 if h else 1),
        ).start()

    def pass_on(part, d, h):
        remote(
            half(part, d, h), q[3 * part].at[0 if d == 1 else 1, pl.ds(2 * h, 2)],
            q_send.at[part, 0], q_recv.at[part, 0], *peer_at(PARTS[part][4][0], d),
        ).start()

    def begin(part):
        halfway(part, 0)
        halfway(part, 1)

    def straight(part):
        pass_on(part, 1, 1)
        pass_on(part, 3, 0)

    def hand_on(part, step, d):
        order = PARTS[part][4]
        remote(
            sums[part].at[(*[own_at[a] for a in order[:step]], share(order[step], d))],
            q[3 * part + step].at[d - 1],
            q_send.at[part, step], q_recv.at[part, step], *peer_at(order[step], d),
        ).start()

    def swap(src, dst, k, kind):
        return remote(src, dst, x_send.at[k, kind], x_recv.at[k, kind], sibling, s)

    def swap_ints(k):
        return swap(bm.at[k, c], bm.at[k, c], k, 0)

    def swap_amps(k):
        return swap(abuf.at[k], sib.at[k], k, 1)

    def clear(n, carry):
        for part in sums:
            part[n] = jnp.zeros(part.shape[1:], F32)
        return carry

    lax.fori_loop(0, 4, clear, 0)

    def contract_chunk(k, carry):
        settle(bbuf.at[k, pl.ds(0, 3), pl.ds(0, SIZE // 8)], b_recv.at[k])
        own_copies(k)[0].wait()

        def mask(t, carry):
            rows = pl.multiple_of(t * 128, 128)
            row_irrep = rowirr[pl.ds(pl.multiple_of(k * SIZE + rows, 128), 128), :]
            for block in range(8):
                n, side = block // 2, block % 2
                part = bbuf[k, n, pl.ds(MARGIN + t * 16, 16), :, pl.ds(side * 128, 128)]
                part = part.astype(F32).reshape(128, 128)
                keep = row_irrep == colirr[0:1, block * 128:block * 128 + 128]
                bm[k, c, pl.ds(rows, 128), block * 128:block * 128 + 128] = jnp.where(
                    keep, part, F32(0)
                ).astype(BF16)
            return carry

        lax.fori_loop(0, SIZE // 128, mask, 0)
        swap_ints(k).start()

        def transpose(w):
            bp[w] = jnp.dot(bm[k, w], perm_ab[...], preferred_element_type=F32).astype(BF16)

        transpose(c)
        settle(abuf.at[k, :, pl.ds(0, 15)], a_recv.at[k])
        for copy in own_copies(k)[1:]:
            copy.wait()
        swap_amps(k).start()
        swap_ints(k).wait_recv()
        transpose(1 - c)
        swap_amps(k).wait_recv()

        for w in range(2):
            mirrored = jnp.dot(
                perm_own[...], abuf[k, w].reshape(512, SIZE), preferred_element_type=F32
            ) + jnp.dot(perm_sib[...], sib[k, w].reshape(512, SIZE), preferred_element_type=F32)
            ap[w] = mirrored.astype(BF16)
        for n in range(NZ):
            cols = slice(n * 256, n * 256 + 256)
            total = None
            for w in range(2):
                for left, right in (
                    (abuf[k, w].reshape(512, SIZE), bm[k, w, :, cols]), (ap[w], bp[w, :, cols])
                ):
                    term = jnp.dot(left, right, preferred_element_type=F32)
                    total = term if total is None else total + term
            total = total.reshape(4, 4, 32, 256)
            for part, (row, rows, lane, lanes, order) in zip(sums, PARTS):
                for i in range(4):
                    for j in range(4):
                        at = {"z": n, "x": i, "y": j}
                        part[tuple(at[a] for a in order)] += total[
                            i, j, row:row + rows, lane:lane + lanes
                        ]
        return carry

    lax.fori_loop(0, NK, contract_chunk, 0)
    for part in range(NP):
        begin(part)
        straight(part)

    def drain(k, carry):
        settle(abuf.at[k, :, pl.ds(0, 15)], a_send)
        settle(bbuf.at[k, pl.ds(0, 3), pl.ds(0, SIZE // 8)], b_send)
        swap_ints(k).wait_send()
        swap_amps(k).wait_send()
        return carry

    lax.fori_loop(0, NK, drain, 0)
    for part in range(NP):
        for h, d in ((0, 1), (1, 3)):
            settle(via[part].at[h], v_recv.at[part, h])
            mine = half(part, d, h)

            mine[...] = mine[...] + via[part][h]
            pass_on(part, d, h)

    for step in range(3):
        for part, (row, rows, lane, lanes, order) in enumerate(PARTS):
            buffer = q[3 * part + step]
            settle(buffer, q_recv.at[part, step])
            mine = sums[part].at[tuple(own_at[a] for a in order[:step + 1])]
            total = mine[...]
            for d in range(3 if step else 2):
                total = total + buffer[d]
            if step == 2:
                fin[pl.ds(row, rows), pl.ds(lane, lanes)] = total
                continue
            mine[...] = total
            for d in (2, 1, 3):
                hand_on(part, step + 1, d)

    fin[...] = fin[...] / den[...]
    for i in range(VS // NZ):
        out[pl.ds(i, 32, stride=VS // NZ), :] = fin[:, i * VS:i * VS + VS]

    for part in range(NP):
        for step in range(3):
            settle(q[3 * part + step], q_send.at[part, step])
        settle(via[part], v_send.at[part])


def contract(amps, ints, irrep, occ, virt):
    dma = pltpu.SemaphoreType.DMA
    scratch = [
        pltpu.VMEM((NK, 2, 16, 32, SIZE), BF16),
        pltpu.VMEM((NK, 2, 16, 32, SIZE), BF16),
        pltpu.VMEM((NK, NZ, SIZE // 8 + 2 * MARGIN, 8, 256), BF16),
        pltpu.VMEM((NK, 2, SIZE, 1024), BF16),
        pltpu.VMEM((2, SIZE, 1024), BF16),
        pltpu.VMEM((2, 512, SIZE), BF16),
        pltpu.VMEM((512, 512), BF16),
        pltpu.VMEM((512, 512), BF16),
        pltpu.VMEM((1024, 1024), BF16),
        pltpu.VMEM((8, 512), F32),
        pltpu.VMEM((LANES, 128), I32),
        pltpu.VMEM((8, 1024), I32),
        pltpu.VMEM((32, 256), F32),
        pltpu.VMEM((32, 256), F32),
        *[pltpu.VMEM((4, 4, 4, rows, lanes), F32) for _, rows, _, lanes, _ in PARTS],
        pltpu.VMEM((1, V), I32),
        pltpu.SMEM((1, OCC), F32),
        pltpu.SMEM((1, VS), F32),
    ]
    for _, rows, _, lanes, _ in PARTS:
        for step, dims in enumerate(STEP_DIMS):
            scratch.append(pltpu.VMEM((3 if step else 2, *dims, rows, lanes), F32))
    scratch += [pltpu.VMEM((2, 2, 4, rows, lanes), F32) for _, rows, _, lanes, _ in PARTS]
    scratch += [
        dma, dma, dma((NK, 2)), dma((NK,)), dma((NK,)), dma((NK, 2)), dma((NK, 3)), dma((3,)),
        dma((NP,)), dma((NP, 2)), dma((NP, 3)), dma((NP, 3)),
    ]
    return pl.pallas_call(
        kernel,
        out_shape=jax.ShapeDtypeStruct((OCC * VS // NZ, VS), F32),
        in_specs=[pl.BlockSpec(memory_space=pltpu.HBM)] * 5,
        out_specs=pl.BlockSpec(memory_space=pltpu.VMEM),
        scratch_shapes=scratch,
        compiler_params=pltpu.CompilerParams(
            collective_id=0, has_side_effects=True, vmem_limit_bytes=64 << 20
        ),
    )(amps, ints, irrep, occ, virt)


def local(amplitudes, integrals, virt_irrep, occ_energy, slab_energy):
    update = contract(
        amplitudes.reshape(OCC, V * V), integrals.reshape(GROUPS, 8, 256),
        virt_irrep.reshape(1, V), occ_energy.reshape(1, OCC), slab_energy.reshape(1, VS),
    )
    return update.reshape(1, OCC, VS // NZ, VS)


def solution(mesh):
    placed = (P("pair", None, None), P("pair", "slab"), P(), P(), P())
    return jax.shard_map(
        local, mesh=mesh, in_specs=placed, out_specs=P("pair", None, "slab", None), check_vma=False
    )
```

```python
import jax
import jax.numpy as jnp
from jax import lax
from jax.experimental import pallas as pl
from jax.experimental.pallas import tpu as pltpu
from jax.sharding import PartitionSpec as P

F32, BF16, I32 = jnp.float32, jnp.bfloat16, jnp.int32
V, VS, OCC = 400, 32, 32
NZ = 4
ROWS = 5000
GROUPS = ROWS // 8
LANES = 1280
SIZE = 256
NK = LANES // SIZE
MARGIN = 16
PARTS = (
    (0, 16, 0, 128, ("z", "x", "y")),
    (0, 16, 128, 128, ("x", "y", "z")),
    (24, 8, 0, 256, ("y", "z", "x")),
    (16, 8, 0, 128, ("z", "x", "y")),
    (16, 8, 128, 128, ("x", "y", "z")),
)
NP = len(PARTS)
STEP_DIMS = ((4, 4), (4,), ())


def shift(i, d, n):
    return lax.rem(i + d, n)


def remote(src, dst, send, recv, pair, slab):
    return pltpu.make_async_remote_copy(
        src_ref=src, dst_ref=dst, send_sem=send, recv_sem=recv,
        device_id={"pair": pair, "slab": slab}, device_id_type=pl.DeviceIdType.MESH,
    )


def settle(ref, sem):
    pltpu.make_async_copy(ref, ref, sem).wait()


def one_hot(test):
    return jnp.where(test, F32(1), F32(0)).astype(BF16)


def kernel(amps, ints, irrep, occ, virt, out, *refs):
    abuf, sib, bbuf, bm, bp = refs[:5]
    refs = refs[5:]
    ap, perm_own, perm_sib, perm_ab, vrow, rowirr, colirr, den, fin = refs[:9]
    sums, refs = refs[9:9 + NP], refs[9 + NP:]
    irrep_v, occ_s, virt_s = refs[:3]
    q, via = refs[3:3 + 3 * NP], refs[3 + 3 * NP:3 + 4 * NP]
    a_send, b_send, x_send, a_recv, b_recv, x_recv, own_sem, arg_sem, v_send, v_recv, q_send, q_recv = (
        refs[3 + 4 * NP:]
    )

    p = lax.axis_index("pair")
    s = lax.axis_index("slab")
    x, y, c = p // 8, lax.rem(p // 2, 4), lax.rem(p, 2)
    place = {"z": s, "x": x, "y": y}
    chip = p // 2
    sibling = p + 1 - 2 * c

    def chip_at(dx, dy):
        return shift(x, dx, 4) * 4 + shift(y, dy, 4)

    barrier = pltpu.get_barrier_semaphore()

    def greet(pair, slab):
        pl.semaphore_signal(
            barrier, inc=1, device_id={"pair": pair, "slab": slab},
            device_id_type=pl.DeviceIdType.MESH,
        )

    def greet_some(dy, carry):
        for dx in (2, 1, 3, 0):
            greet(chip_at(dx, dy + dx) * 2 + c, s)
        return carry

    for dx in (2, 1, 3):
        greet(chip_at(dx, dx) * 2 + c, s)
    lax.fori_loop(1, 4, greet_some, 0)
    for dz in (2, 1, 3):
        greet(p, shift(s, dz, NZ))
    greet(sibling, s)
    small = [
        pltpu.make_async_copy(src, dst, arg_sem.at[i])
        for i, (src, dst) in enumerate(((irrep, irrep_v), (occ, occ_s), (virt, virt_s)))
    ]
    for copy in small:
        copy.start()
    pl.semaphore_wait(barrier, 19)

    first_tile = ROWS * p // 128
    lead = lax.rem(p, 16)

    def columns(pair, k):
        tile = ROWS * pair // 128 + 10 * s
        return pl.ds(pl.multiple_of(tile * 128 + k * SIZE, 128), SIZE)

    def rows_for(slab, k):
        want = 160 * slab - lead + k * (SIZE // 8)
        have = jnp.clip(want, 0, GROUPS - SIZE // 8)
        return pl.ds(have, SIZE // 8), pl.ds(MARGIN + have - want, SIZE // 8)

    def own_copies(k):
        source, target = rows_for(s, k)
        return [
            pltpu.make_async_copy(ints.at[source], bbuf.at[k, 3, target], own_sem.at[k, 2]),
        ] + [
            pltpu.make_async_copy(
                amps.at[:, columns(chip * 2 + w, k)], abuf.at[k, w, chip], own_sem.at[k, w]
            )
            for w in range(2)
        ]

    def send_amps(k, dx, dy, w):
        peer = chip_at(dx, dy) * 2
        remote(
            amps.at[:, columns(peer + w, k)], abuf.at[k, w, chip], a_send, a_recv.at[k, w], peer + c, s
        ).start()

    def send_chunk(k, carry):
        for dz in (1, 3, 2):
            slab = shift(s, dz, NZ)
            source, target = rows_for(slab, k)
            remote(
                ints.at[source], bbuf.at[k, 3 - dz, target], b_send, b_recv.at[k], p, slab
            ).start()
        def send_range(w, carry):
            for dx in (1, 3, 2):
                send_amps(k, dx, dx, w)

            def send_some(dy, carry):
                for dx in (1, 3, 2, 0):
                    send_amps(k, dx, dy + dx, w)
                return carry

            return lax.fori_loop(1, 4, send_some, carry)

        lax.fori_loop(0, 2, send_range, 0)
        for copy in own_copies(k):
            copy.start()
        return carry

    lax.fori_loop(0, NK, send_chunk, 0)

    def orbitals(col):
        return ((((col >> 8) + s + 1) & 3) << 3) | ((col >> 5) & 7), col & 31

    def fill_perm(t, carry):
        row = lax.broadcasted_iota(I32, (128, 1024), 0) + t * 128
        col = lax.broadcasted_iota(I32, (128, 1024), 1)
        rows = pl.ds(pl.multiple_of(t * 128, 128), 128)
        a, b = orbitals(col)
        perm_ab[rows, :] = one_hot(
            row == (((((b >> 3) + 3 - s) & 3) << 8) | ((b & 7) << 5) | a)
        )
        return carry

    lax.fori_loop(0, 8, fill_perm, 0)

    def fill_swap(t, carry):
        row = lax.broadcasted_iota(I32, (128, 512), 0) + t * 128
        col = lax.broadcasted_iota(I32, (128, 512), 1)
        rows = pl.ds(pl.multiple_of(t * 128, 128), 128)
        i, j = ((row >> 5) << 1) + c, row & 31
        here = (((j >> 1) << 5) | i) == col
        perm_own[rows, :] = one_hot(here & ((j & 1) == c))
        perm_sib[rows, :] = one_hot(here & ((j & 1) != c))
        return carry

    lax.fori_loop(0, 4, fill_swap, 0)
    for copy in small:
        copy.wait()

    vrow[...] = jnp.zeros_like(vrow)
    vrow[0:1, 0:V] = irrep_v[...].astype(F32)
    table = jnp.broadcast_to(vrow[0:1, :], (128, 512)).astype(BF16)

    def look_up(lhs, rhs, dims):
        return lax.dot_general(
            lhs, rhs, (dims, ((), ())), preferred_element_type=F32
        ).astype(I32)

    orb = lax.broadcasted_iota(I32, (128, 1024), 0)
    col = lax.broadcasted_iota(I32, (128, 1024), 1)
    first = table[0:16, 0:128]
    of_a, of_b = (look_up(first, one_hot(orb == v), ((1,), (0,))) for v in orbitals(col))
    colirr[...] = (of_a ^ of_b)[0:8]

    start = (first_tile + 10 * s) * 128

    def fill_rows(t, carry):
        base = start + t * 256
        c0 = base // V
        row = lax.broadcasted_iota(I32, (256, 512), 0) + base
        orb = lax.broadcasted_iota(I32, (256, 512), 1)
        cc = jnp.where(row >= (c0 + 1) * V, c0 + 1, c0)
        of_c = look_up(one_hot(orb == cc), table, ((1,), (1,)))
        of_d = look_up(one_hot(orb == row - cc * V), table, ((1,), (1,)))
        row = row[:, 0:128]
        inside = (row >= ROWS * p) & (row < ROWS * p + ROWS)
        rowirr[pl.ds(pl.multiple_of(t * 256, 256), 256), :] = jnp.where(inside, of_c ^ of_d, -1)
        return carry

    lax.fori_loop(0, LANES // 256, fill_rows, 0)

    lane = lax.broadcasted_iota(I32, (8, 256), 1)
    row = lax.broadcasted_iota(I32, (32, 256), 0)
    of_a = jnp.zeros((8, 256), F32)
    of_b = jnp.zeros((8, 256), F32)
    of_j = jnp.zeros((32, 256), F32)
    for i in range(VS // NZ):
        of_a = jnp.where((lane >> 5) == i, virt_s[0, s * (VS // NZ) + i], of_a)
    for i in range(VS):
        of_b = jnp.where((lane & 31) == i, virt_s[0, i], of_b)
    for i in range(OCC):
        of_j = jnp.where(row == i, occ_s[0, i], of_j)
    den[...] = ((of_a + of_b) - occ_s[0, p])[0:1] - of_j

    own_at = {"z": 3, "x": x, "y": y}

    def peer_at(axis, d):
        at = {**place, axis: shift(place[axis], d, 4)}
        return at["x"] * 8 + at["y"] * 2 + c, at["z"]

    def share(axis, d):
        return d - 1 if axis == "z" else shift(place[axis], d, 4)

    def half(part, d, h):
        return sums[part].at[share(PARTS[part][4][0], d), pl.ds(2 * h, 2)]

    def halfway(part, h):
        remote(
            half(part, 2, h), via[part].at[h], v_send.at[part], v_recv.at[part, h],
            *peer_at(PARTS[part][4][0], 3 if h else 1),
        ).start()

    def pass_on(part, d, h):
        remote(
            half(part, d, h), q[3 * part].at[0 if d == 1 else 1, pl.ds(2 * h, 2)],
            q_send.at[part, 0], q_recv.at[part, 0], *peer_at(PARTS[part][4][0], d),
        ).start()

    def begin(part):
        halfway(part, 0)
        halfway(part, 1)

    def straight(part):
        pass_on(part, 1, 1)
        pass_on(part, 3, 0)

    def hand_on(part, step, d):
        order = PARTS[part][4]
        remote(
            sums[part].at[(*[own_at[a] for a in order[:step]], share(order[step], d))],
            q[3 * part + step].at[d - 1],
            q_send.at[part, step], q_recv.at[part, step], *peer_at(order[step], d),
        ).start()

    def swap(src, dst, k, kind):
        return remote(src, dst, x_send.at[k, kind], x_recv.at[k, kind], sibling, s)

    def swap_ints(k):
        return swap(bm.at[k, c], bm.at[k, c], k, 0)

    def swap_amps(k, w):
        return swap(abuf.at[k, w], sib.at[k, w], k, 1 + w)

    def clear(n, carry):
        for part in sums:
            part[n] = jnp.zeros(part.shape[1:], F32)
        return carry

    lax.fori_loop(0, 4, clear, 0)

    def contract_chunk(k, carry):
        settle(bbuf.at[k, pl.ds(0, 3), pl.ds(0, SIZE // 8)], b_recv.at[k])
        own_copies(k)[0].wait()

        def mask(t, carry):
            rows = pl.multiple_of(t * 128, 128)
            row_irrep = rowirr[pl.ds(pl.multiple_of(k * SIZE + rows, 128), 128), :]
            for block in range(8):
                n, side = block // 2, block % 2
                part = bbuf[k, n, pl.ds(MARGIN + t * 16, 16), :, pl.ds(side * 128, 128)]
                part = part.astype(F32).reshape(128, 128)
                keep = row_irrep == colirr[0:1, block * 128:block * 128 + 128]
                bm[k, c, pl.ds(rows, 128), block * 128:block * 128 + 128] = jnp.where(
                    keep, part, F32(0)
                ).astype(BF16)
            return carry

        lax.fori_loop(0, SIZE // 128, mask, 0, unroll=True)
        swap_ints(k).start()

        def transpose(w):
            bp[w] = jnp.dot(bm[k, w], perm_ab[...], preferred_element_type=F32).astype(BF16)

        transpose(c)
        own = own_copies(k)[1:]
        for w in range(2):
            settle(abuf.at[k, w, pl.ds(0, 15)], a_recv.at[k, w])
            own[w].wait()
            swap_amps(k, w).start()
        swap_ints(k).wait_recv()
        transpose(1 - c)
        swap_amps(k, 0).wait_recv()
        swap_amps(k, 1).wait_recv()

        for w in range(2):
            mirrored = jnp.dot(
                perm_own[...], abuf[k, w].reshape(512, SIZE), preferred_element_type=F32
            ) + jnp.dot(perm_sib[...], sib[k, w].reshape(512, SIZE), preferred_element_type=F32)
            ap[w] = mirrored.astype(BF16)
        for n in range(NZ):
            cols = slice(n * 256, n * 256 + 256)
            total = None
            for w in range(2):
                for left, right in (
                    (abuf[k, w].reshape(512, SIZE), bm[k, w, :, cols]), (ap[w], bp[w, :, cols])
                ):
                    term = jnp.dot(left, right, preferred_element_type=F32)
                    total = term if total is None else total + term
            total = total.reshape(4, 4, 32, 256)
            for part, (row, rows, lane, lanes, order) in zip(sums, PARTS):
                for i in range(4):
                    for j in range(4):
                        at = {"z": n, "x": i, "y": j}
                        part[tuple(at[a] for a in order)] += total[
                            i, j, row:row + rows, lane:lane + lanes
                        ]
        return carry

    lax.fori_loop(0, NK, contract_chunk, 0)
    for part in range(NP):
        begin(part)
    for part in range(NP):
        straight(part)

    def drain(k, carry):
        settle(abuf.at[k, :, pl.ds(0, 15)], a_send)
        settle(bbuf.at[k, pl.ds(0, 3), pl.ds(0, SIZE // 8)], b_send)
        swap_ints(k).wait_send()
        swap_amps(k, 0).wait_send()
        swap_amps(k, 1).wait_send()
        return carry

    lax.fori_loop(0, NK, drain, 0)
    for part in range(NP):
        for h, d in ((0, 1), (1, 3)):
            settle(via[part].at[h], v_recv.at[part, h])
            mine = half(part, d, h)

            mine[...] = mine[...] + via[part][h]
            pass_on(part, d, h)

    for step in range(3):
        for part, (row, rows, lane, lanes, order) in enumerate(PARTS):
            buffer = q[3 * part + step]
            settle(buffer, q_recv.at[part, step])
            mine = sums[part].at[tuple(own_at[a] for a in order[:step + 1])]
            total = mine[...]
            for d in range(3 if step else 2):
                total = total + buffer[d]
            if step == 2:
                fin[pl.ds(row, rows), pl.ds(lane, lanes)] = total
                continue
            mine[...] = total
            for d in (2, 1, 3):
                hand_on(part, step + 1, d)

    fin[...] = fin[...] / den[...]
    for i in range(VS // NZ):
        out[pl.ds(i, 32, stride=VS // NZ), :] = fin[:, i * VS:i * VS + VS]

    for part in range(NP):
        for step in range(3):
            settle(q[3 * part + step], q_send.at[part, step])
        settle(via[part], v_send.at[part])


def contract(amps, ints, irrep, occ, virt):
    dma = pltpu.SemaphoreType.DMA
    scratch = [
        pltpu.VMEM((NK, 2, 16, 32, SIZE), BF16),
        pltpu.VMEM((NK, 2, 16, 32, SIZE), BF16),
        pltpu.VMEM((NK, NZ, SIZE // 8 + 2 * MARGIN, 8, 256), BF16),
        pltpu.VMEM((NK, 2, SIZE, 1024), BF16),
        pltpu.VMEM((2, SIZE, 1024), BF16),
        pltpu.VMEM((2, 512, SIZE), BF16),
        pltpu.VMEM((512, 512), BF16),
        pltpu.VMEM((512, 512), BF16),
        pltpu.VMEM((1024, 1024), BF16),
        pltpu.VMEM((8, 512), F32),
        pltpu.VMEM((LANES, 128), I32),
        pltpu.VMEM((8, 1024), I32),
        pltpu.VMEM((32, 256), F32),
        pltpu.VMEM((32, 256), F32),
        *[pltpu.VMEM((4, 4, 4, rows, lanes), F32) for _, rows, _, lanes, _ in PARTS],
        pltpu.VMEM((1, V), I32),
        pltpu.SMEM((1, OCC), F32),
        pltpu.SMEM((1, VS), F32),
    ]
    for _, rows, _, lanes, _ in PARTS:
        for step, dims in enumerate(STEP_DIMS):
            scratch.append(pltpu.VMEM((3 if step else 2, *dims, rows, lanes), F32))
    scratch += [pltpu.VMEM((2, 2, 4, rows, lanes), F32) for _, rows, _, lanes, _ in PARTS]
    scratch += [
        dma, dma, dma((NK, 3)), dma((NK, 2)), dma((NK,)), dma((NK, 3)), dma((NK, 3)), dma((3,)),
        dma((NP,)), dma((NP, 2)), dma((NP, 3)), dma((NP, 3)),
    ]
    return pl.pallas_call(
        kernel,
        out_shape=jax.ShapeDtypeStruct((OCC * VS // NZ, VS), F32),
        in_specs=[pl.BlockSpec(memory_space=pltpu.HBM)] * 5,
        out_specs=pl.BlockSpec(memory_space=pltpu.VMEM),
        scratch_shapes=scratch,
        compiler_params=pltpu.CompilerParams(
            collective_id=0, has_side_effects=True, vmem_limit_bytes=64 << 20
        ),
    )(amps, ints, irrep, occ, virt)


def local(amplitudes, integrals, virt_irrep, occ_energy, slab_energy):
    update = contract(
        amplitudes.reshape(OCC, V * V), integrals.reshape(GROUPS, 8, 256),
        virt_irrep.reshape(1, V), occ_energy.reshape(1, OCC), slab_energy.reshape(1, VS),
    )
    return update.reshape(1, OCC, VS // NZ, VS)


def solution(mesh):
    placed = (P("pair", None, None), P("pair", "slab"), P(), P(), P())
    return jax.shard_map(
        local, mesh=mesh, in_specs=placed, out_specs=P("pair", None, "slab", None), check_vma=False
    )
```

```python
import jax
import jax.numpy as jnp
from jax import lax
from jax.experimental import pallas as pl
from jax.experimental.pallas import tpu as pltpu
from jax.sharding import PartitionSpec as P

F32, BF16, I32 = jnp.float32, jnp.bfloat16, jnp.int32
V, VS, OCC = 400, 32, 32
NZ = 4
ROWS = 5000
GROUPS = ROWS // 8
LANES = 1280
SIZE = 256
NK = LANES // SIZE
MARGIN = 16
PARTS = (
    (0, 16, 0, 128, ("z", "x", "y")),
    (0, 16, 128, 128, ("x", "y", "z")),
    (24, 8, 0, 128, ("y", "z", "x")),
    (16, 8, 0, 128, ("z", "x", "y")),
    (16, 8, 128, 128, ("x", "y", "z")),
    (24, 8, 128, 128, ("y", "z", "x")),
)
NP = len(PARTS)
STEP_DIMS = ((4, 4), (4,), ())


def shift(i, d, n):
    return lax.rem(i + d, n)


def remote(src, dst, send, recv, pair, slab):
    return pltpu.make_async_remote_copy(
        src_ref=src, dst_ref=dst, send_sem=send, recv_sem=recv,
        device_id={"pair": pair, "slab": slab}, device_id_type=pl.DeviceIdType.MESH,
    )


def settle(ref, sem):
    pltpu.make_async_copy(ref, ref, sem).wait()


def one_hot(test):
    return jnp.where(test, F32(1), F32(0)).astype(BF16)


def kernel(amps, ints, irrep, occ, virt, out, *refs):
    abuf, sib, bbuf, bm, bp = refs[:5]
    refs = refs[5:]
    ap, perm_own, perm_sib, perm_ab, vrow, rowirr, colirr, den, fin = refs[:9]
    sums, refs = refs[9:9 + NP], refs[9 + NP:]
    irrep_v, occ_s, virt_s = refs[:3]
    q, via = refs[3:3 + 3 * NP], refs[3 + 3 * NP:3 + 4 * NP]
    a_send, b_send, x_send, a_recv, b_recv, x_recv, own_sem, arg_sem, v_send, v_recv, q_send, q_recv = (
        refs[3 + 4 * NP:]
    )

    p = lax.axis_index("pair")
    s = lax.axis_index("slab")
    x, y, c = p // 8, lax.rem(p // 2, 4), lax.rem(p, 2)
    place = {"z": s, "x": x, "y": y}
    chip = p // 2
    sibling = p + 1 - 2 * c

    def chip_at(dx, dy):
        return shift(x, dx, 4) * 4 + shift(y, dy, 4)

    barrier = pltpu.get_barrier_semaphore()

    def greet(pair, slab):
        pl.semaphore_signal(
            barrier, inc=1, device_id={"pair": pair, "slab": slab},
            device_id_type=pl.DeviceIdType.MESH,
        )

    def greet_some(dy, carry):
        for dx in (2, 1, 3, 0):
            greet(chip_at(dx, dy + dx) * 2 + c, s)
        return carry

    for dx in (2, 1, 3):
        greet(chip_at(dx, dx) * 2 + c, s)
    lax.fori_loop(1, 4, greet_some, 0)
    for dz in (2, 1, 3):
        greet(p, shift(s, dz, NZ))
    greet(sibling, s)
    small = [
        pltpu.make_async_copy(src, dst, arg_sem.at[i])
        for i, (src, dst) in enumerate(((irrep, irrep_v), (occ, occ_s), (virt, virt_s)))
    ]
    for copy in small:
        copy.start()
    pl.semaphore_wait(barrier, 19)

    first_tile = ROWS * p // 128
    lead = lax.rem(p, 16)

    def columns(pair, k):
        tile = ROWS * pair // 128 + 10 * s
        return pl.ds(pl.multiple_of(tile * 128 + k * SIZE, 128), SIZE)

    def rows_for(slab, k):
        want = 160 * slab - lead + k * (SIZE // 8)
        have = jnp.clip(want, 0, GROUPS - SIZE // 8)
        return pl.ds(have, SIZE // 8), pl.ds(MARGIN + have - want, SIZE // 8)

    def own_copies(k):
        source, target = rows_for(s, k)
        return [
            pltpu.make_async_copy(ints.at[source], bbuf.at[k, 3, target], own_sem.at[k, 2]),
        ] + [
            pltpu.make_async_copy(
                amps.at[:, columns(chip * 2 + w, k)], abuf.at[k, w, chip], own_sem.at[k, w]
            )
            for w in range(2)
        ]

    def send_amps(k, dx, dy, w):
        peer = chip_at(dx, dy) * 2
        remote(
            amps.at[:, columns(peer + w, k)], abuf.at[k, w, chip], a_send, a_recv.at[k, w], peer + c, s
        ).start()

    def send_chunk(k, carry):
        for dz in (1, 3, 2):
            slab = shift(s, dz, NZ)
            source, target = rows_for(slab, k)
            remote(
                ints.at[source], bbuf.at[k, 3 - dz, target], b_send, b_recv.at[k], p, slab
            ).start()
        def send_range(w, carry):
            for dx in (1, 3, 2):
                send_amps(k, dx, dx, w)

            def send_some(dy, carry):
                for dx in (1, 3, 2, 0):
                    send_amps(k, dx, dy + dx, w)
                return carry

            return lax.fori_loop(1, 4, send_some, carry)

        lax.fori_loop(0, 2, send_range, 0)
        for copy in own_copies(k):
            copy.start()
        return carry

    lax.fori_loop(0, NK, send_chunk, 0)

    def orbitals(col):
        return ((((col >> 8) + s + 1) & 3) << 3) | ((col >> 5) & 7), col & 31

    def fill_perm(t, carry):
        row = lax.broadcasted_iota(I32, (128, 1024), 0) + t * 128
        col = lax.broadcasted_iota(I32, (128, 1024), 1)
        rows = pl.ds(pl.multiple_of(t * 128, 128), 128)
        a, b = orbitals(col)
        perm_ab[rows, :] = one_hot(
            row == (((((b >> 3) + 3 - s) & 3) << 8) | ((b & 7) << 5) | a)
        )
        return carry

    lax.fori_loop(0, 8, fill_perm, 0)

    def fill_swap(t, carry):
        row = lax.broadcasted_iota(I32, (128, 512), 0) + t * 128
        col = lax.broadcasted_iota(I32, (128, 512), 1)
        rows = pl.ds(pl.multiple_of(t * 128, 128), 128)
        i, j = ((row >> 5) << 1) + c, row & 31
        here = (((j >> 1) << 5) | i) == col
        perm_own[rows, :] = one_hot(here & ((j & 1) == c))
        perm_sib[rows, :] = one_hot(here & ((j & 1) != c))
        return carry

    lax.fori_loop(0, 4, fill_swap, 0)
    for copy in small:
        copy.wait()

    vrow[...] = jnp.zeros_like(vrow)
    vrow[0:1, 0:V] = irrep_v[...].astype(F32)
    table = jnp.broadcast_to(vrow[0:1, :], (128, 512)).astype(BF16)

    def look_up(lhs, rhs, dims):
        return lax.dot_general(
            lhs, rhs, (dims, ((), ())), preferred_element_type=F32
        ).astype(I32)

    orb = lax.broadcasted_iota(I32, (128, 1024), 0)
    col = lax.broadcasted_iota(I32, (128, 1024), 1)
    first = table[0:16, 0:128]
    of_a, of_b = (look_up(first, one_hot(orb == v), ((1,), (0,))) for v in orbitals(col))
    colirr[...] = (of_a ^ of_b)[0:8]

    start = (first_tile + 10 * s) * 128

    def fill_rows(t, carry):
        base = start + t * 256
        c0 = base // V
        row = lax.broadcasted_iota(I32, (256, 512), 0) + base
        orb = lax.broadcasted_iota(I32, (256, 512), 1)
        cc = jnp.where(row >= (c0 + 1) * V, c0 + 1, c0)
        of_c = look_up(one_hot(orb == cc), table, ((1,), (1,)))
        of_d = look_up(one_hot(orb == row - cc * V), table, ((1,), (1,)))
        row = row[:, 0:128]
        inside = (row >= ROWS * p) & (row < ROWS * p + ROWS)
        rowirr[pl.ds(pl.multiple_of(t * 256, 256), 256), :] = jnp.where(inside, of_c ^ of_d, -1)
        return carry

    lax.fori_loop(0, LANES // 256, fill_rows, 0)

    lane = lax.broadcasted_iota(I32, (8, 256), 1)
    row = lax.broadcasted_iota(I32, (32, 256), 0)
    of_a = jnp.zeros((8, 256), F32)
    of_b = jnp.zeros((8, 256), F32)
    of_j = jnp.zeros((32, 256), F32)
    for i in range(VS // NZ):
        of_a = jnp.where((lane >> 5) == i, virt_s[0, s * (VS // NZ) + i], of_a)
    for i in range(VS):
        of_b = jnp.where((lane & 31) == i, virt_s[0, i], of_b)
    for i in range(OCC):
        of_j = jnp.where(row == i, occ_s[0, i], of_j)
    den[...] = ((of_a + of_b) - occ_s[0, p])[0:1] - of_j

    own_at = {"z": 3, "x": x, "y": y}

    def peer_at(axis, d):
        at = {**place, axis: shift(place[axis], d, 4)}
        return at["x"] * 8 + at["y"] * 2 + c, at["z"]

    def share(axis, d):
        return d - 1 if axis == "z" else shift(place[axis], d, 4)

    def half(part, d, h):
        return sums[part].at[share(PARTS[part][4][0], d), pl.ds(2 * h, 2)]

    def halfway(part, h):
        remote(
            half(part, 2, h), via[part].at[h], v_send.at[part], v_recv.at[part, h],
            *peer_at(PARTS[part][4][0], 3 if h else 1),
        ).start()

    def pass_on(part, d, h):
        remote(
            half(part, d, h), q[3 * part].at[0 if d == 1 else 1, pl.ds(2 * h, 2)],
            q_send.at[part, 0], q_recv.at[part, 0], *peer_at(PARTS[part][4][0], d),
        ).start()

    def begin(part):
        halfway(part, 0)
        halfway(part, 1)

    def straight(part):
        pass_on(part, 1, 1)
        pass_on(part, 3, 0)

    def hand_on(part, step, d):
        order = PARTS[part][4]
        remote(
            sums[part].at[(*[own_at[a] for a in order[:step]], share(order[step], d))],
            q[3 * part + step].at[d - 1],
            q_send.at[part, step], q_recv.at[part, step], *peer_at(order[step], d),
        ).start()

    def swap(src, dst, k, kind):
        return remote(src, dst, x_send.at[k, kind], x_recv.at[k, kind], sibling, s)

    def swap_ints(k):
        return swap(bm.at[k, c], bm.at[k, c], k, 0)

    def swap_amps(k, w):
        return swap(abuf.at[k, w], sib.at[k, w], k, 1 + w)

    def clear(n, carry):
        for part in sums:
            part[n] = jnp.zeros(part.shape[1:], F32)
        return carry

    lax.fori_loop(0, 4, clear, 0)

    def contract_chunk(k, carry):
        settle(bbuf.at[k, pl.ds(0, 3), pl.ds(0, SIZE // 8)], b_recv.at[k])
        own_copies(k)[0].wait()

        def mask(t, carry):
            rows = pl.multiple_of(t * 128, 128)
            row_irrep = rowirr[pl.ds(pl.multiple_of(k * SIZE + rows, 128), 128), :]
            for block in range(8):
                n, side = block // 2, block % 2
                part = bbuf[k, n, pl.ds(MARGIN + t * 16, 16), :, pl.ds(side * 128, 128)]
                part = part.astype(F32).reshape(128, 128)
                keep = row_irrep == colirr[0:1, block * 128:block * 128 + 128]
                bm[k, c, pl.ds(rows, 128), block * 128:block * 128 + 128] = jnp.where(
                    keep, part, F32(0)
                ).astype(BF16)
            return carry

        lax.fori_loop(0, SIZE // 128, mask, 0, unroll=True)
        swap_ints(k).start()

        def transpose(w):
            bp[w] = jnp.dot(bm[k, w], perm_ab[...], preferred_element_type=F32).astype(BF16)

        transpose(c)
        own = own_copies(k)[1:]
        for w in range(2):
            settle(abuf.at[k, w, pl.ds(0, 15)], a_recv.at[k, w])
            own[w].wait()
            swap_amps(k, w).start()
        swap_ints(k).wait_recv()
        transpose(1 - c)
        swap_amps(k, 0).wait_recv()
        swap_amps(k, 1).wait_recv()

        for w in range(2):
            mirrored = jnp.dot(
                perm_own[...], abuf[k, w].reshape(512, SIZE), preferred_element_type=F32
            ) + jnp.dot(perm_sib[...], sib[k, w].reshape(512, SIZE), preferred_element_type=F32)
            ap[w] = mirrored.astype(BF16)
        for n in range(NZ):
            cols = slice(n * 256, n * 256 + 256)
            total = None
            for w in range(2):
                for left, right in (
                    (abuf[k, w].reshape(512, SIZE), bm[k, w, :, cols]), (ap[w], bp[w, :, cols])
                ):
                    term = jnp.dot(left, right, preferred_element_type=F32)
                    total = term if total is None else total + term
            total = total.reshape(4, 4, 32, 256)
            for part, (row, rows, lane, lanes, order) in zip(sums, PARTS):
                for i in range(4):
                    for j in range(4):
                        at = {"z": n, "x": i, "y": j}
                        part[tuple(at[a] for a in order)] += total[
                            i, j, row:row + rows, lane:lane + lanes
                        ]
        return carry

    lax.fori_loop(0, NK, contract_chunk, 0)
    for part in range(NP):
        begin(part)
    for part in range(NP):
        straight(part)

    def drain(k, carry):
        settle(abuf.at[k, :, pl.ds(0, 15)], a_send)
        settle(bbuf.at[k, pl.ds(0, 3), pl.ds(0, SIZE // 8)], b_send)
        swap_ints(k).wait_send()
        swap_amps(k, 0).wait_send()
        swap_amps(k, 1).wait_send()
        return carry

    lax.fori_loop(0, NK, drain, 0)
    for part in range(NP):
        for h, d in ((0, 1), (1, 3)):
            settle(via[part].at[h], v_recv.at[part, h])
            mine = half(part, d, h)

            mine[...] = mine[...] + via[part][h]
            pass_on(part, d, h)

    for step in range(3):
        for part, (row, rows, lane, lanes, order) in enumerate(PARTS):
            buffer = q[3 * part + step]
            settle(buffer, q_recv.at[part, step])
            mine = sums[part].at[tuple(own_at[a] for a in order[:step + 1])]
            total = mine[...]
            for d in range(3 if step else 2):
                total = total + buffer[d]
            if step == 2:
                fin[pl.ds(row, rows), pl.ds(lane, lanes)] = total
                continue
            mine[...] = total
            for d in (2, 1, 3):
                hand_on(part, step + 1, d)

    fin[...] = fin[...] / den[...]
    for i in range(VS // NZ):
        out[pl.ds(i, 32, stride=VS // NZ), :] = fin[:, i * VS:i * VS + VS]

    for part in range(NP):
        for step in range(3):
            settle(q[3 * part + step], q_send.at[part, step])
        settle(via[part], v_send.at[part])


def contract(amps, ints, irrep, occ, virt):
    dma = pltpu.SemaphoreType.DMA
    scratch = [
        pltpu.VMEM((NK, 2, 16, 32, SIZE), BF16),
        pltpu.VMEM((NK, 2, 16, 32, SIZE), BF16),
        pltpu.VMEM((NK, NZ, SIZE // 8 + 2 * MARGIN, 8, 256), BF16),
        pltpu.VMEM((NK, 2, SIZE, 1024), BF16),
        pltpu.VMEM((2, SIZE, 1024), BF16),
        pltpu.VMEM((2, 512, SIZE), BF16),
        pltpu.VMEM((512, 512), BF16),
        pltpu.VMEM((512, 512), BF16),
        pltpu.VMEM((1024, 1024), BF16),
        pltpu.VMEM((8, 512), F32),
        pltpu.VMEM((LANES, 128), I32),
        pltpu.VMEM((8, 1024), I32),
        pltpu.VMEM((32, 256), F32),
        pltpu.VMEM((32, 256), F32),
        *[pltpu.VMEM((4, 4, 4, rows, lanes), F32) for _, rows, _, lanes, _ in PARTS],
        pltpu.VMEM((1, V), I32),
        pltpu.SMEM((1, OCC), F32),
        pltpu.SMEM((1, VS), F32),
    ]
    for _, rows, _, lanes, _ in PARTS:
        for step, dims in enumerate(STEP_DIMS):
            scratch.append(pltpu.VMEM((3 if step else 2, *dims, rows, lanes), F32))
    scratch += [pltpu.VMEM((2, 2, 4, rows, lanes), F32) for _, rows, _, lanes, _ in PARTS]
    scratch += [
        dma, dma, dma((NK, 3)), dma((NK, 2)), dma((NK,)), dma((NK, 3)), dma((NK, 3)), dma((3,)),
        dma((NP,)), dma((NP, 2)), dma((NP, 3)), dma((NP, 3)),
    ]
    return pl.pallas_call(
        kernel,
        out_shape=jax.ShapeDtypeStruct((OCC * VS // NZ, VS), F32),
        in_specs=[pl.BlockSpec(memory_space=pltpu.HBM)] * 5,
        out_specs=pl.BlockSpec(memory_space=pltpu.VMEM),
        scratch_shapes=scratch,
        compiler_params=pltpu.CompilerParams(
            collective_id=0, has_side_effects=True, vmem_limit_bytes=64 << 20
        ),
    )(amps, ints, irrep, occ, virt)


def local(amplitudes, integrals, virt_irrep, occ_energy, slab_energy):
    update = contract(
        amplitudes.reshape(OCC, V * V), integrals.reshape(GROUPS, 8, 256),
        virt_irrep.reshape(1, V), occ_energy.reshape(1, OCC), slab_energy.reshape(1, VS),
    )
    return update.reshape(1, OCC, VS // NZ, VS)


def solution(mesh):
    placed = (P("pair", None, None), P("pair", "slab"), P(), P(), P())
    return jax.shard_map(
        local, mesh=mesh, in_specs=placed, out_specs=P("pair", None, "slab", None), check_vma=False
    )
```
